32 devices in a mesh: section: 4 (over x, core), seq: 8 (over z, y).
Axes of the slice: x: 2, y: 2, z: 4, core: 2. Of those that a mesh axis runs over, the one named last changes fastest.
Arguments:
- layer_input: bfloat16 [4, 512, 4, 1536], P('section', 'seq'), may hold values from -300 to 300
- norm_gain: float32 [4, 1536], P('section'), may hold values from 0.1 to 1.9
- queries: bfloat16 [4, 512, 4, 1024], P('section', 'seq'), may hold values from -6 to 6
- key_states: bfloat16 [4, 512, 4, 1024], P('section', 'seq'), may hold values from -6 to 6
- value_states: bfloat16 [4, 512, 4, 1024], P('section', 'seq'), may hold values from -6 to 6
- out_grad: bfloat16 [4, 512, 4, 1536], P('section', 'seq'), may hold values from -6 to 6
- out_weight: bfloat16 [4, 1024, 1536], P('section', 'seq'), may hold values from -0.1875 to 0.1875
- qkv_weight: bfloat16 [4, 1536, 3072], P('section', 'seq'), may hold values from -0.15625 to 0.15625
- lengths: int32 [4, 4], P('section'), may hold values from 256 to 512
Outputs:
- passed_grad: bfloat16 [4, 512, 4, 1536], P('section', 'seq')
The draws below stay inside these ranges and needn't reach their ends.
All inputs are finite; a program needn't handle non-finite values.
Results may differ from the reference program's by a relative error of at most 0.0034.
Values may be sent and summed in bfloat16 or wider, within the bound.
A program may use at most 128 MiB of HBM per device.

```python
import jax
import jax.numpy as jnp
from jax import lax

D = 1536
HEADS = 16
HS = 64
SEQS = 4
SECTIONS = 4
L = 512


def draw_queries(key, part):
    values = jnp.clip(1.5 * jax.random.normal(jax.random.fold_in(key, 21), (SECTIONS, L, SEQS, HEADS * HS), jnp.float32), -6.0, 6.0)
    return values.astype(jnp.bfloat16)


def draw_key_states(key, part):
    values = jnp.clip(1.5 * jax.random.normal(jax.random.fold_in(key, 22), (SECTIONS, L, SEQS, HEADS * HS), jnp.float32), -6.0, 6.0)
    return values.astype(jnp.bfloat16)


def draw_layer_input(key, part):
    values = jnp.clip(jax.random.normal(jax.random.fold_in(key, 31), (SECTIONS, L, SEQS, D), jnp.float32), -6.0, 6.0)
    return values.astype(jnp.bfloat16)


def with_ends(values, stream_key, least, high):
    spot = [jax.random.randint(jax.random.fold_in(stream_key, axis), (), 0, length) for axis, length in enumerate(values.shape)]
    widest = values.shape.index(max(values.shape))
    next_to = spot[:widest] + [(spot[widest] + 1) % values.shape[widest]] + spot[widest + 1:]
    return values.at[tuple(spot)].set(least).at[tuple(next_to)].set(high)


def steps_of(stream_key, extent, cuts, least, high):
    level = 1.0
    for axis_at, blocks in cuts:
        draws = jax.random.uniform(jax.random.fold_in(jax.random.fold_in(stream_key, 6), axis_at), (blocks,), jnp.float32, least / len(cuts), high / len(cuts))
        level = level * jnp.repeat(jnp.exp(draws), extent[axis_at] // blocks).reshape((-1,) + (1,) * (len(extent) - 1 - axis_at))
    return level


def gaussian(rng, extent, scale, bound, shards=(), held_as=jnp.bfloat16):
    entries = jax.random.normal(rng, extent, jnp.float32) * scale
    if len(shards) > 0:
        entries = steps_of(rng, extent, shards, -0.22, 0.18) * entries
    return jnp.clip(entries, min=-bound, max=bound).astype(held_as)


def setup_inputs(seed: int = 0) -> dict:
    splits = jax.random.split(jax.random.key(seed), 10)
    return {
        "layer_input": draw_layer_input(jax.random.fold_in(splits[9], 71), 0),
        "norm_gain": jnp.clip(1.0 + 0.18 * jax.random.normal(splits[1], (SECTIONS, D), jnp.float32), 0.1, 1.9),
        "queries": draw_queries(jax.random.fold_in(splits[9], 71), 0),
        "key_states": draw_key_states(jax.random.fold_in(splits[9], 71), 0),
        "value_states": gaussian(splits[4], (SECTIONS, L, SEQS, HEADS * HS), 1.0, 6.0, ((0, 4), (1, 8))),
        "out_grad": gaussian(splits[5], (SECTIONS, L, SEQS, D), 1.0, 6.0, ((0, 4), (1, 8))),
        "out_weight": gaussian(splits[6], (SECTIONS, HEADS * HS, D), (HEADS * HS) ** -0.5, 0.1875, ((0, 4), (1, 8))),
        "qkv_weight": gaussian(splits[7], (SECTIONS, D, 3 * HEADS * HS), D ** -0.5, 0.15625, ((0, 4), (1, 8))),
        "lengths": with_ends(jax.random.randint(splits[8], (SECTIONS, SEQS), L // 2, L + 1), jax.random.fold_in(splits[8], 1), L // 2, L).astype(jnp.int32),
    }


EPSILON = 1e-05
MASKED = -1e+30

def item_backward(query_rows, key_rows, value_rows, grad_rows, key_valid):
    length = query_rows.shape[0]
    block = min(512, length)
    scale = HS ** (-0.5)
    offsets = jnp.arange(0, length, block).astype(jnp.int32)
    zeros = jnp.zeros((length, query_rows.shape[1]), jnp.float32)

    def step(carry, offset):
        key_total, value_total = carry
        query_block = lax.dynamic_slice_in_dim(query_rows, offset, block, 0)
        grad_block = lax.dynamic_slice_in_dim(grad_rows, offset, block, 0)
        scores = jnp.dot(query_block, key_rows.T, preferred_element_type=jnp.float32) * scale
        scores = jnp.where(key_valid[None, :], scores, MASKED)
        largest = lax.optimization_barrier(jnp.max(scores, axis=1, keepdims=True))
        weights = jnp.exp(scores - largest)
        probs = weights / lax.optimization_barrier(jnp.sum(weights, axis=1, keepdims=True))
        probs_low = probs.astype(jnp.bfloat16)
        grad_probs = jnp.dot(grad_block, value_rows.T, preferred_element_type=jnp.float32)
        centre = lax.optimization_barrier(jnp.sum(probs * grad_probs, axis=1, keepdims=True))
        grad_scores = (probs * (grad_probs - centre) * scale).astype(jnp.bfloat16)
        query_grad = jnp.dot(grad_scores, key_rows, preferred_element_type=jnp.float32)
        key_total = key_total + jnp.dot(grad_scores.T, query_block, preferred_element_type=jnp.float32)
        value_total = value_total + jnp.dot(probs_low.T, grad_block, preferred_element_type=jnp.float32)
        return ((key_total, value_total), query_grad.astype(jnp.bfloat16))
    (key_total, value_total), query_parts = lax.scan(step, (zeros, zeros), offsets)
    query_grad = query_parts.reshape(length, query_rows.shape[1])
    return (query_grad, key_total.astype(jnp.bfloat16), value_total.astype(jnp.bfloat16))

def to_items(array):
    return array.reshape(L, SEQS, HEADS, HS).transpose(1, 2, 0, 3).reshape(SEQS * HEADS, L, HS)

def from_items(array):
    return array.reshape(SEQS, HEADS, L, HS).transpose(2, 0, 1, 3).reshape(L * SEQS, HEADS * HS)

def section_backward(operands):
    layer_input, norm_gain, queries, key_states, value_states, out_grad, out_weight, qkv_weight, lengths = operands
    flat_grad = out_grad.reshape(L * SEQS, D)
    attn_grad = jnp.dot(flat_grad, out_weight.T, preferred_element_type=jnp.float32).astype(jnp.bfloat16)
    attn_grad = attn_grad.reshape(L, SEQS, HEADS * HS)
    positions = jnp.arange(L).astype(jnp.int32)
    valid = positions[None, :] < lengths[:, None]
    valid_items = jnp.repeat(valid, HEADS, axis=0)
    query_grad, key_gradient, value_grad = lax.map(lambda group: item_backward(*group), (to_items(queries), to_items(key_states), to_items(value_states), to_items(attn_grad), valid_items))
    joined = jnp.concatenate([from_items(query_grad), from_items(key_gradient), from_items(value_grad)], axis=1)
    norm_grad = jnp.dot(joined, qkv_weight.T, preferred_element_type=jnp.float32)
    inputs = layer_input.reshape(L * SEQS, D).astype(jnp.float32)
    row_average = lax.optimization_barrier(jnp.mean(inputs, axis=1, keepdims=True))
    centered_input = inputs - row_average
    var = lax.optimization_barrier(jnp.mean(centered_input * centered_input, axis=1, keepdims=True))
    inverse_deviation = 1.0 / jnp.sqrt(var + EPSILON)
    normalized_input = centered_input * inverse_deviation
    scaled_rows = norm_grad * norm_gain[None, :]
    residual_branch = inverse_deviation * (scaled_rows - lax.optimization_barrier(jnp.mean(scaled_rows, axis=1, keepdims=True)) - normalized_input * lax.optimization_barrier(jnp.mean(scaled_rows * normalized_input, axis=1, keepdims=True)))
    input_grad = (flat_grad.astype(jnp.float32) + residual_branch).astype(jnp.bfloat16)
    return input_grad.reshape(L, SEQS, D)

def reference(layer_input, norm_gain, queries, key_states, value_states, out_grad, out_weight, qkv_weight, lengths):
    input_grad = lax.map(section_backward, (layer_input, norm_gain, queries, key_states, value_states, out_grad, out_weight, qkv_weight, lengths))
    return jnp.roll(input_grad, -1, axis=0)
```

```python
import functools

import jax
import jax.numpy as jnp
from jax import lax
from jax.experimental import pallas as pl
from jax.experimental.pallas import tpu as pltpu
from jax.sharding import PartitionSpec as P

HEADS = 16
HS = 64


EPSILON = 1e-05
MASKED = -1e30
ROW_DOT = (((1,), (1,)), ((), ()))
COL_DOT = (((0,), (0,)), ((), ()))


def shifted(shard, axis, by):
    count = lax.axis_size(axis)
    return lax.ppermute(shard, axis, [(i, (i + by) % count) for i in range(count)])


def item_backward(query_rows, key_rows, value_rows, grad_rows, key_valid):
    length = query_rows.shape[0]
    block = min(512, length)
    scale = HS ** (-0.5)
    offsets = jnp.arange(0, length, block)
    zeros = jnp.zeros((length, query_rows.shape[1]), jnp.float32)

    def step(carry, offset):
        key_total, value_total = carry
        query_block = lax.dynamic_slice_in_dim(query_rows, offset, block, 0)
        grad_block = lax.dynamic_slice_in_dim(grad_rows, offset, block, 0)
        scores = (
            lax.dot_general(query_block, key_rows, ROW_DOT, preferred_element_type=jnp.float32)
            * scale
        )
        scores = jnp.where(key_valid[None, :], scores, MASKED)
        largest = jnp.max(scores, axis=1, keepdims=True)
        weights = jnp.exp(scores - largest)
        probs = weights / jnp.sum(weights, axis=1, keepdims=True)
        probs_low = probs.astype(jnp.bfloat16)
        grad_probs = lax.dot_general(
            grad_block, value_rows, ROW_DOT, preferred_element_type=jnp.float32
        )
        centre = jnp.sum(probs * grad_probs, axis=1, keepdims=True)
        grad_scores = (probs * (grad_probs - centre) * scale).astype(jnp.bfloat16)
        query_grad = jnp.dot(grad_scores, key_rows, preferred_element_type=jnp.float32)
        key_total = key_total + lax.dot_general(
            grad_scores, query_block, COL_DOT, preferred_element_type=jnp.float32
        )
        value_total = value_total + lax.dot_general(
            probs_low, grad_block, COL_DOT, preferred_element_type=jnp.float32
        )
        return ((key_total, value_total), query_grad.astype(jnp.bfloat16))

    (key_total, value_total), query_parts = lax.scan(step, (zeros, zeros), offsets)
    query_grad = query_parts.reshape(length, query_rows.shape[1])
    return (query_grad, key_total.astype(jnp.bfloat16), value_total.astype(jnp.bfloat16))


def split_items(columns):
    length = columns.shape[0]
    count = columns.shape[1] // HS
    return columns.reshape(length, count, HS).transpose(1, 0, 2)


def join_items(items):
    count = items.shape[0]
    length = items.shape[1]
    return items.transpose(1, 0, 2).reshape(length, count * HS)


def project_grad(flat_grad, out_rows):
    return lax.dot_general(
        flat_grad,
        lax.all_gather(out_rows, "seq", axis=0, tiled=True),
        ROW_DOT,
        preferred_element_type=jnp.float32,
    ).astype(jnp.bfloat16)


def on_device(
    layer_input,
    norm_gain,
    queries,
    key_states,
    value_states,
    out_grad,
    out_weight,
    qkv_weight,
    lengths,
):
    frames = queries.shape[1]
    records = queries.shape[2]
    features = queries.shape[3]
    model_width = out_grad.shape[3]
    flat_grad = out_grad[0].reshape(frames * records, model_width)
    frame_queries = queries[0].reshape(frames, records * features)
    frame_keys = key_states[0].reshape(frames, records * features)
    frame_values = value_states[0].reshape(frames, records * features)
    attn_grad = project_grad(flat_grad, out_weight[0])
    head_queries, head_keys, head_values, head_grads = (
        lax.all_to_all(frame_queries, "seq", split_axis=1, concat_axis=0, tiled=True),
        lax.all_to_all(frame_keys, "seq", split_axis=1, concat_axis=0, tiled=True),
        lax.all_to_all(frame_values, "seq", split_axis=1, concat_axis=0, tiled=True),
        lax.all_to_all(
            attn_grad.reshape(frames, records * features),
            "seq",
            split_axis=1,
            concat_axis=0,
            tiled=True,
        ),
    )
    items_here = head_queries.shape[1] // HS
    length = head_queries.shape[0]
    item_ids = lax.axis_index("seq") * items_here + jnp.arange(items_here, dtype=jnp.int32)
    record_ids = item_ids // HEADS
    record_pick = jnp.arange(records, dtype=jnp.int32)[None, :] == record_ids[:, None]
    item_lengths = jnp.sum(jnp.where(record_pick, lengths[0][None, :], 0), axis=1)
    key_valid = jnp.arange(length, dtype=jnp.int32)[None, :] < item_lengths[:, None]
    query_grad, key_gradient, value_grad = lax.map(
        lambda group: item_backward(*group),
        (
            split_items(head_queries),
            split_items(head_keys),
            split_items(head_values),
            split_items(head_grads),
            key_valid,
        ),
    )
    query_back, key_backward, value_back = (
        lax.all_to_all(join_items(query_grad), "seq", split_axis=0, concat_axis=1, tiled=True),
        lax.all_to_all(join_items(key_gradient), "seq", split_axis=0, concat_axis=1, tiled=True),
        lax.all_to_all(join_items(value_grad), "seq", split_axis=0, concat_axis=1, tiled=True),
    )
    joined = jnp.concatenate(
        [
            query_back.reshape(frames * records, features),
            key_backward.reshape(frames * records, features),
            value_back.reshape(frames * records, features),
        ],
        axis=1,
    )
    norm_grad = lax.dot_general(
        joined,
        lax.all_gather(qkv_weight[0], "seq", axis=0, tiled=True),
        ROW_DOT,
        preferred_element_type=jnp.float32,
    )
    inputs = layer_input[0].reshape(frames * records, model_width).astype(jnp.float32)
    row_average = jnp.mean(inputs, axis=1, keepdims=True)
    centered_input = inputs - row_average
    var = jnp.mean(centered_input * centered_input, axis=1, keepdims=True)
    inverse_deviation = 1.0 / jnp.sqrt(var + EPSILON)
    normalized_input = centered_input * inverse_deviation
    scaled_rows = norm_grad * norm_gain[0][None, :]
    residual_branch = inverse_deviation * (
        scaled_rows
        - jnp.mean(scaled_rows, axis=1, keepdims=True)
        - normalized_input * jnp.mean(scaled_rows * normalized_input, axis=1, keepdims=True)
    )
    input_grad = (flat_grad.astype(jnp.float32) + residual_branch).astype(jnp.bfloat16)
    input_grad = input_grad.reshape(1, frames, records, model_width)
    return shifted(input_grad, "section", -1)


def body(
    dims,
    length_ref,
    li_ref,
    q_ref,
    k_ref,
    v_ref,
    og_ref,
    ow_in,
    w_in,
    gain_ref,
    out_ref,
    xq,
    xk,
    xv,
    xo,
    g,
    ow,
    w,
    joined,
    part_send,
    side_recv,
    sum_send,
    part_recv,
    li_here,
    og_here,
    lens,
    gains,
    x_send_sem,
    x_recv_sem,
    o_send_sem,
    o_pass_sem,
    o_recv_sem,
    ow_send_sem,
    ow_pass_sem,
    ow_recv_sem,
    w_send_sem,
    w_pass_sem,
    w_recv_sem,
    side_send_sem,
    side_recv_sem,
    p_send_sem,
    p_recv_sem,
    s_send_sem,
    s_recv_sem,
    twin_send_sem,
    twin_recv_sem,
):
    n, sections, records, parts, frames, cols = dims
    pairs = cols // (2 * HS)
    section = lax.axis_index("section")
    me = lax.axis_index("seq")
    core = section % 2
    z = me // parts
    part = me % parts
    half = z // 2
    twin = section + 1 - 2 * core
    work = section - core + half
    record = 2 * (z % 2) + core
    lead = core == half
    near = z == 1 + half
    prior = (section + sections - 1) % sections
    before = (work + sections - 1) % sections

    def remote(src, dst, send, recv, sec, dev):
        return pltpu.make_async_remote_copy(
            src_ref=src,
            dst_ref=dst,
            send_sem=send,
            recv_sem=recv,
            device_id=(sec, dev),
            device_id_type=pl.DeviceIdType.MESH,
        )

    def either(stays, copy_here, copy_there):
        @pl.when(stays)
        def _():
            copy_here().start()

        @pl.when(jnp.logical_not(stays))
        def _():
            copy_there().start()

    barrier = pltpu.get_barrier_semaphore()
    for s in range(sections):
        for k in range(n):
            if s or k:
                pl.semaphore_signal(
                    barrier,
                    inc=1,
                    device_id=((section + s) % sections, (me + k) % n),
                    device_id_type=pl.DeviceIdType.MESH,
                )

    lane = lax.broadcasted_iota(jnp.int32, lens.shape[1:], 1)
    lengths = jnp.zeros(lens.shape[1:], jnp.int32)
    for r in range(records):
        lengths = jnp.where(lane == r, length_ref[r], lengths)
    lens[0] = lengths

    pl.semaphore_wait(barrier, sections * n - 1)

    twin_lens = remote(lens.at[0], lens.at[1], twin_send_sem.at[0], twin_recv_sem.at[0], twin, me)
    twin_gain = remote(gain_ref, gains, twin_send_sem.at[1], twin_recv_sem.at[1], twin, me)

    def seat(r, p):
        return section - core + r % 2, (2 * core + r // 2) * parts + p

    def turn(i):
        return (i + 2 * core) % records

    heads = [(q_ref, xq), (k_ref, xk), (v_ref, xv)]

    def x_source(t, r, p):
        return heads[t][0].at[r, :, pl.ds(p * cols, cols)]

    def x_copy(t, i, p):
        r = turn(i)
        sec, dev = seat(r, p)
        return remote(
            x_source(t, r, p),
            heads[t][1].at[me],
            x_send_sem.at[t, i, p],
            x_recv_sem.at[t, me],
            sec,
            dev,
        )

    def x_stays(i, p):
        return lead & (turn(i) == record) & (part == p)

    def x_start(t):
        for i in range(records):
            for p in range(parts):
                either(
                    x_stays(i, p),
                    lambda: pltpu.make_async_copy(
                        x_source(t, turn(i), p), heads[t][1].at[me], x_recv_sem.at[t, me]
                    ),
                    lambda: x_copy(t, i, p),
                )

    def og_source(r):
        return og_ref.at[pl.ds(pl.multiple_of(r * frames, frames), frames)]

    def o_copy(i):
        r = turn(i)
        sec, dev = seat(r, part)
        return remote(og_source(r), xo.at[me], o_send_sem.at[i], o_recv_sem.at[me], sec, dev)

    def o_stays(i):
        return lead & (turn(i) == record)

    def o_pass(k):
        slot = k * parts + part
        return remote(
            xo.at[slot],
            xo.at[slot],
            o_pass_sem.at[k],
            o_recv_sem.at[slot],
            section,
            z * parts + 1 - part,
        )

    def lead_z(d):
        return 1 + core if d == 0 else 3 * core

    ow_slot = me % records

    def ow_copy(d):
        return remote(
            ow_in,
            ow.at[ow_slot],
            ow_send_sem.at[d],
            ow_recv_sem.at[ow_slot],
            section,
            lead_z(d) * parts + half,
        )

    def ow_stays(d):
        return (lead_z(d) == z) & (part == half)

    def w_source(t, p):
        return w_in.at[:, pl.ds((t * parts + p) * cols, cols)]

    def w_target(t):
        return w.at[me, :, pl.ds(t * cols, cols)]

    def w_copy(d, p, t):
        return remote(
            w_source(t, p),
            w_target(t),
            w_send_sem.at[d, p, t],
            w_recv_sem.at[me],
            section,
            lead_z(d) * parts + p,
        )

    def w_stays(d, p):
        return (lead_z(d) == z) & (part == p)

    def sends(d):
        return lead | (d == 0)

    def ow_start(d):
        either(
            ow_stays(d),
            lambda: pltpu.make_async_copy(ow_in, ow.at[ow_slot], ow_recv_sem.at[ow_slot]),
            lambda: ow_copy(d),
        )

    def w_start(d):
        for p in range(parts):
            for t in range(3):
                either(
                    w_stays(d, p),
                    lambda: pltpu.make_async_copy(w_source(t, p), w_target(t), w_recv_sem.at[me]),
                    lambda: w_copy(d, p, t),
                )

    def both_leads(start):
        start(0)

        @pl.when(lead)
        def _():
            start(1)

    def ow_on(slot, way):
        sec, dev = (twin, me) if way == 0 else (section, 3 * half * parts + part)
        return remote(
            ow.at[slot], ow.at[slot], ow_pass_sem.at[way, slot], ow_recv_sem.at[slot], sec, dev
        )

    def w_on(slot, way):
        sec, dev = (twin, me) if way == 0 else (section, 3 * half * parts + part)
        return remote(
            w.at[slot], w.at[slot], w_pass_sem.at[way, slot], w_recv_sem.at[slot], sec, dev
        )

    ow_relays = lead & near & (part != half)

    def w_relays(origin):
        return lead & near & (origin // 2 != half)

    def w_pass(origin):
        for other in range(parts):
            slot = origin * parts + other
            w_on(slot, 0).wait_recv()

            @pl.when(w_relays(origin))
            def _():
                w_on(slot, 1).start()

            @pl.when(lead)
            def _():
                w_on(slot, 0).start()

    def order(i):
        return (z, 2 * half + 1 - z % 2, 2 - half, 3 - 3 * half)[i]

    shift_og = remote(og_ref, og_here, s_send_sem.at[0], s_recv_sem.at[0], prior, me)
    shift_li = remote(li_ref, li_here, s_send_sem.at[1], s_recv_sem.at[1], prior, me)

    twin_lens.start()
    twin_gain.start()
    both_leads(ow_start)
    for i in range(records):
        r = turn(i)
        either(
            o_stays(i),
            lambda: pltpu.make_async_copy(og_source(r), xo.at[me], o_recv_sem.at[me]),
            lambda: o_copy(i),
        )
    for t in range(3):
        x_start(t)
    shift_og.start()
    shift_li.start()

    for slot in range(records):
        ow_on(slot, 0).wait_recv()

        @pl.when(ow_relays)
        def _():
            ow_on(slot, 1).start()

        @pl.when(lead)
        def _():
            ow_on(slot, 0).start()

    for k in range(records):
        o_pass(k).wait_recv()
        o_pass(k).start()
    both_leads(w_start)
    for k in range(records):
        slot = k * parts + 1 - part
        remote(
            xo.at[slot], xo.at[slot], o_pass_sem.at[k], o_recv_sem.at[slot], section, me
        ).wait_recv()

    length = n * frames
    rows_here = ow.shape[1]

    def project(i, carry):
        weight = ow[pl.ds(2 * i, 2)].reshape(2 * rows_here, ow.shape[2])
        grads = xo[...].reshape(length, xo.shape[2])
        lanes = pl.ds(pl.multiple_of(i * 2 * rows_here, 2 * rows_here), 2 * rows_here)
        g[:, lanes] = lax.dot_general(
            grads, weight, ROW_DOT, preferred_element_type=jnp.float32
        ).astype(jnp.bfloat16)
        return carry

    lax.fori_loop(0, cols // (2 * rows_here), project, 0)
    twin_lens.wait_recv()
    twin_gain.wait_recv()
    for t in range(3):
        for j in range(n):
            remote(
                heads[t][1].at[j],
                heads[t][1].at[j],
                x_send_sem.at[t, 0, 0],
                x_recv_sem.at[t, j],
                section,
                me,
            ).wait_recv()

    valid = jnp.where(lead, lens[0], lens[1])
    valid = jnp.sum(jnp.where(lane == record, valid, 0), axis=1, keepdims=True)[:1]
    keys_ok = lax.broadcasted_iota(jnp.int32, (length, 1), 0) < valid
    low_lanes = lax.broadcasted_iota(jnp.int32, (length, 2 * HS), 1) < HS
    scale = HS ** (-0.5)

    def attend(j, carry):
        lanes = pl.ds(pl.multiple_of(j * 2 * HS, 2 * HS), 2 * HS)
        queries, keys, values = (x[:, :, lanes].reshape(length, 2 * HS) for x in (xq, xk, xv))
        grads = g[:, lanes]
        keys_across = keys.T
        nothing = jnp.zeros_like(keys)
        halves = []
        for h in range(2):
            mine = low_lanes if h == 0 else jnp.logical_not(low_lanes)
            key_h = jnp.where(mine, keys, nothing)
            value_h = jnp.where(mine, values, nothing)
            scores = (
                lax.dot_general(key_h, queries, ROW_DOT, preferred_element_type=jnp.float32)
                * scale
            )
            scores = jnp.where(keys_ok, scores, MASKED)
            weights = jnp.exp(scores - jnp.max(scores, axis=0, keepdims=True))
            probs = weights * (1.0 / jnp.sum(weights, axis=0, keepdims=True))
            grad_probs = lax.dot_general(
                value_h, grads, ROW_DOT, preferred_element_type=jnp.float32
            )
            centre = jnp.sum(probs * grad_probs, axis=0, keepdims=True)
            grad_scores = (probs * (grad_probs - centre)).astype(jnp.bfloat16)
            value_grad = jnp.dot(
                probs.astype(jnp.bfloat16), grads, preferred_element_type=jnp.float32
            )
            key_grad = jnp.dot(grad_scores, queries, preferred_element_type=jnp.float32)
            query_grad = jnp.dot(
                keys_across[h * HS : (h + 1) * HS], grad_scores, preferred_element_type=jnp.float32
            )
            halves.append((query_grad, key_grad, value_grad))
        (query_0, key_0, value_0), (query_1, key_1, value_1) = halves
        query_both = (jnp.concatenate([query_0, query_1], axis=0) * scale).T
        key_both = jnp.where(low_lanes, key_0, key_1) * scale
        value_both = jnp.where(low_lanes, value_0, value_1)
        for t, both in enumerate((query_both, key_both, value_both)):
            at = pl.multiple_of(t * cols + j * 2 * HS, 2 * HS)
            joined[:, pl.ds(at, 2 * HS)] = both.astype(jnp.bfloat16)

        for i in range(records - 1):

            @pl.when(j == max(pairs - (records - 1) + i, 0))
            def _():
                w_pass(order(i))

        return carry

    lax.fori_loop(0, pairs, attend, 0)

    def side_copy(origin):
        other = 1 - part
        return remote(
            part_send.at[origin, other],
            side_recv.at[origin],
            side_send_sem.at[origin],
            side_recv_sem.at[origin],
            section,
            z * parts + other,
        )

    def sum_copy(origin, to):
        return remote(
            sum_send.at[origin, to],
            part_recv.at[record, origin],
            p_send_sem.at[origin, to],
            p_recv_sem.at[record, origin],
            before,
            to * parts + part,
        )

    def sum_stays(to):
        return (before == section) & (to == z)

    def norm_block(origin):
        weight = w[pl.ds(origin * parts, parts)].reshape(parts * w.shape[1], w.shape[2])
        sums = lax.dot_general(
            joined[...], weight, ROW_DOT, preferred_element_type=jnp.float32
        )
        gain = jnp.where(lead, gain_ref[origin], gains[origin])
        sums = (sums * gain).astype(jnp.bfloat16)
        sums = sums.reshape(records, parts, frames, sums.shape[1])
        for other in range(parts):
            part_send[origin, other] = sums[:, other]
        side_copy(origin).start()

    def norm_send(origin):
        side_copy(origin).wait_recv()
        total = part_send[origin, part].astype(jnp.float32)
        total = total + side_recv[origin].astype(jnp.float32)
        sum_send[origin] = total.astype(jnp.bfloat16)
        for k in range(records):
            to = (z + k) % records
            either(
                sum_stays(to),
                lambda: pltpu.make_async_copy(
                    sum_send.at[origin, to],
                    part_recv.at[record, origin],
                    p_recv_sem.at[record, origin],
                ),
                lambda: sum_copy(origin, to),
            )

    def norm(i, carry):
        origin = jnp.where(
            i == 0, order(0), jnp.where(i == 1, order(1), jnp.where(i == 2, order(2), order(3)))
        )
        last = jnp.where(i == 1, order(0), jnp.where(i == 2, order(1), order(2)))

        @pl.when(i == records - 1)
        def _():
            norm_send(last)
            w_pass(origin)

        norm_block(origin)

        @pl.when((i > 0) & (i < records - 1))
        def _():
            norm_send(last)

        @pl.when(i == records - 1)
        def _():
            norm_send(origin)

        return carry

    lax.fori_loop(0, records, norm, 0)

    shift_og.wait_recv()
    shift_li.wait_recv()
    for src in range(records):
        for origin in range(records):
            remote(
                sum_send.at[origin, 0],
                part_recv.at[src, origin],
                p_send_sem.at[origin, 0],
                p_recv_sem.at[src, origin],
                before,
                me,
            ).wait_recv()

    width = og_here.shape[1]

    def finish(r):
        rows = pl.ds(r * frames, frames)
        inputs = li_here[:, r, :].astype(jnp.float32)
        centered = inputs - jnp.sum(inputs, axis=1, keepdims=True) * (1.0 / width)
        var = jnp.sum(centered * centered, axis=1, keepdims=True) * (1.0 / width)
        deviation = 1.0 / jnp.sqrt(var + EPSILON)
        normal = centered * deviation
        scaled = []
        for origin in range(records):
            scaled.append(part_recv[r, origin].astype(jnp.float32))
        scaled = jnp.concatenate(scaled, axis=1)
        average = jnp.sum(scaled, axis=1, keepdims=True) * (1.0 / width)
        along = jnp.sum(scaled * normal, axis=1, keepdims=True) * (1.0 / width)
        branch = deviation * (scaled - average - normal * along)
        out_ref[rows, :] = (og_here[rows, :].astype(jnp.float32) + branch).astype(jnp.bfloat16)

    for r in range(records):
        finish(r)

    def sent(stays, copy):
        @pl.when(jnp.logical_not(stays))
        def _():
            copy.wait_send()

    twin_lens.wait_send()
    twin_gain.wait_send()
    shift_og.wait_send()
    shift_li.wait_send()
    for i in range(records):
        sent(o_stays(i), o_copy(i))
        o_pass(i).wait_send()
        for t in range(3):
            for p in range(parts):
                sent(x_stays(i, p), x_copy(t, i, p))
    for d in range(2):

        @pl.when(sends(d))
        def _():
            sent(ow_stays(d), ow_copy(d))
            for p in range(parts):
                for t in range(3):
                    sent(w_stays(d, p), w_copy(d, p, t))

    @pl.when(ow_relays)
    def _():
        for slot in range(records):
            ow_on(slot, 1).wait_send()

    @pl.when(lead)
    def _():
        for slot in range(records):
            ow_on(slot, 0).wait_send()
        for slot in range(n):
            w_on(slot, 0).wait_send()

    for origin in range(records):

        @pl.when(w_relays(origin))
        def _():
            for other in range(parts):
                w_on(origin * parts + other, 1).wait_send()

        side_copy(origin).wait_send()
        for to in range(records):
            sent(sum_stays(to), sum_copy(origin, to))


def on_device_fused(
    layer_input,
    norm_gain,
    queries,
    key_states,
    value_states,
    out_grad,
    out_weight,
    qkv_weight,
    lengths,
):
    n = lax.axis_size("seq")
    sections = lax.axis_size("section")
    frames, records, features = queries.shape[1:]
    width = out_grad.shape[3]
    parts = n // records
    cols = features // parts
    ow_rows = out_weight.shape[1]
    w_rows = qkv_weight.shape[1]
    block = parts * w_rows

    def by_record(x):
        return x[0].transpose(1, 0, 2)

    flat_grad = by_record(out_grad).reshape(records * frames, width)
    gain = norm_gain[0].reshape(records, 1, block)
    vmem = pl.BlockSpec(memory_space=pltpu.VMEM)
    low = jnp.bfloat16
    dma = pltpu.SemaphoreType.DMA
    out = pl.pallas_call(
        functools.partial(body, (n, sections, records, parts, frames, cols)),
        out_shape=jax.ShapeDtypeStruct((records * frames, width), low),
        in_specs=[pl.BlockSpec(memory_space=pltpu.SMEM)] + [vmem] * 8,
        out_specs=vmem,
        scratch_shapes=[pltpu.VMEM((n, frames, cols), low)] * 3
        + [
            pltpu.VMEM((n, frames, width), low),
            pltpu.VMEM((n * frames, cols), low),
            pltpu.VMEM((records, ow_rows, width), low),
            pltpu.VMEM((n, w_rows, 3 * cols), low),
            pltpu.VMEM((n * frames, 3 * cols), low),
            pltpu.VMEM((records, parts, records, frames, block), low),
            pltpu.VMEM((records, records, frames, block), low),
            pltpu.VMEM((records, records, frames, block), low),
            pltpu.VMEM((records, records, frames, block), low),
            pltpu.VMEM((frames, records, width), low),
            pltpu.VMEM((records * frames, width), low),
            pltpu.VMEM((2, 8, 128), jnp.int32),
            pltpu.VMEM((records, 1, block), jnp.float32),
            dma((3, records, parts)),
            dma((3, n)),
            dma((records,)),
            dma((records,)),
            dma((n,)),
            dma((2,)),
            dma((2, records)),
            dma((records,)),
            dma((2, parts, 3)),
            dma((2, n)),
            dma((n,)),
            dma((records,)),
            dma((records,)),
            dma((records, records)),
            dma((records, records)),
            dma((2,)),
            dma((2,)),
            dma((2,)),
            dma((2,)),
        ],
        compiler_params=pltpu.CompilerParams(
            collective_id=0, has_side_effects=True, vmem_limit_bytes=60 * 1024 * 1024
        ),
    )(
        lengths[0],
        layer_input[0],
        by_record(queries),
        by_record(key_states),
        by_record(value_states),
        flat_grad,
        out_weight[0],
        qkv_weight[0],
        gain,
    )
    return out.reshape(records, frames, width).transpose(1, 0, 2)[None]


def fits(mesh, records, features):
    n = mesh.shape["seq"]
    if n != 2 * records or records != 4 or mesh.shape["section"] % 2:
        return False
    return features % (n * HS) == 0


def solution(mesh):
    in_specs = (
        P("section", "seq", None, None),
        P("section", None),
        P("section", "seq", None, None),
        P("section", "seq", None, None),
        P("section", "seq", None, None),
        P("section", "seq", None, None),
        P("section", "seq", None),
        P("section", "seq", None),
        P("section", None),
    )
    out_specs = P("section", "seq", None, None)

    def run(*arrays):
        fused = fits(mesh, arrays[2].shape[2], arrays[2].shape[3])
        return jax.shard_map(
            on_device_fused if fused else on_device,
            mesh=mesh,
            in_specs=in_specs,
            out_specs=out_specs,
            check_vma=False,
        )(*arrays)

    return run
```

```python
import functools

import jax
import jax.numpy as jnp
from jax import lax
from jax.experimental import pallas as pl
from jax.experimental.pallas import tpu as pltpu
from jax.sharding import PartitionSpec as P

HEADS = 16
HS = 64


EPSILON = 1e-05
MASKED = -1e30
ROW_DOT = (((1,), (1,)), ((), ()))
COL_DOT = (((0,), (0,)), ((), ()))


def shifted(shard, axis, by):
    count = lax.axis_size(axis)
    return lax.ppermute(shard, axis, [(i, (i + by) % count) for i in range(count)])


def item_backward(query_rows, key_rows, value_rows, grad_rows, key_valid):
    length = query_rows.shape[0]
    block = min(512, length)
    scale = HS ** (-0.5)
    offsets = jnp.arange(0, length, block)
    zeros = jnp.zeros((length, query_rows.shape[1]), jnp.float32)

    def step(carry, offset):
        key_total, value_total = carry
        query_block = lax.dynamic_slice_in_dim(query_rows, offset, block, 0)
        grad_block = lax.dynamic_slice_in_dim(grad_rows, offset, block, 0)
        scores = (
            lax.dot_general(query_block, key_rows, ROW_DOT, preferred_element_type=jnp.float32)
            * scale
        )
        scores = jnp.where(key_valid[None, :], scores, MASKED)
        largest = jnp.max(scores, axis=1, keepdims=True)
        weights = jnp.exp(scores - largest)
        probs = weights / jnp.sum(weights, axis=1, keepdims=True)
        probs_low = probs.astype(jnp.bfloat16)
        grad_probs = lax.dot_general(
            grad_block, value_rows, ROW_DOT, preferred_element_type=jnp.float32
        )
        centre = jnp.sum(probs * grad_probs, axis=1, keepdims=True)
        grad_scores = (probs * (grad_probs - centre) * scale).astype(jnp.bfloat16)
        query_grad = jnp.dot(grad_scores, key_rows, preferred_element_type=jnp.float32)
        key_total = key_total + lax.dot_general(
            grad_scores, query_block, COL_DOT, preferred_element_type=jnp.float32
        )
        value_total = value_total + lax.dot_general(
            probs_low, grad_block, COL_DOT, preferred_element_type=jnp.float32
        )
        return ((key_total, value_total), query_grad.astype(jnp.bfloat16))

    (key_total, value_total), query_parts = lax.scan(step, (zeros, zeros), offsets)
    query_grad = query_parts.reshape(length, query_rows.shape[1])
    return (query_grad, key_total.astype(jnp.bfloat16), value_total.astype(jnp.bfloat16))


def split_items(columns):
    length = columns.shape[0]
    count = columns.shape[1] // HS
    return columns.reshape(length, count, HS).transpose(1, 0, 2)


def join_items(items):
    count = items.shape[0]
    length = items.shape[1]
    return items.transpose(1, 0, 2).reshape(length, count * HS)


def project_grad(flat_grad, out_rows):
    return lax.dot_general(
        flat_grad,
        lax.all_gather(out_rows, "seq", axis=0, tiled=True),
        ROW_DOT,
        preferred_element_type=jnp.float32,
    ).astype(jnp.bfloat16)


def on_device(
    layer_input,
    norm_gain,
    queries,
    key_states,
    value_states,
    out_grad,
    out_weight,
    qkv_weight,
    lengths,
):
    frames = queries.shape[1]
    records = queries.shape[2]
    features = queries.shape[3]
    model_width = out_grad.shape[3]
    flat_grad = out_grad[0].reshape(frames * records, model_width)
    frame_queries = queries[0].reshape(frames, records * features)
    frame_keys = key_states[0].reshape(frames, records * features)
    frame_values = value_states[0].reshape(frames, records * features)
    attn_grad = project_grad(flat_grad, out_weight[0])
    head_queries, head_keys, head_values, head_grads = (
        lax.all_to_all(frame_queries, "seq", split_axis=1, concat_axis=0, tiled=True),
        lax.all_to_all(frame_keys, "seq", split_axis=1, concat_axis=0, tiled=True),
        lax.all_to_all(frame_values, "seq", split_axis=1, concat_axis=0, tiled=True),
        lax.all_to_all(
            attn_grad.reshape(frames, records * features),
            "seq",
            split_axis=1,
            concat_axis=0,
            tiled=True,
        ),
    )
    items_here = head_queries.shape[1] // HS
    length = head_queries.shape[0]
    item_ids = lax.axis_index("seq") * items_here + jnp.arange(items_here, dtype=jnp.int32)
    record_ids = item_ids // HEADS
    record_pick = jnp.arange(records, dtype=jnp.int32)[None, :] == record_ids[:, None]
    item_lengths = jnp.sum(jnp.where(record_pick, lengths[0][None, :], 0), axis=1)
    key_valid = jnp.arange(length, dtype=jnp.int32)[None, :] < item_lengths[:, None]
    query_grad, key_gradient, value_grad = lax.map(
        lambda group: item_backward(*group),
        (
            split_items(head_queries),
            split_items(head_keys),
            split_items(head_values),
            split_items(head_grads),
            key_valid,
        ),
    )
    query_back, key_backward, value_back = (
        lax.all_to_all(join_items(query_grad), "seq", split_axis=0, concat_axis=1, tiled=True),
        lax.all_to_all(join_items(key_gradient), "seq", split_axis=0, concat_axis=1, tiled=True),
        lax.all_to_all(join_items(value_grad), "seq", split_axis=0, concat_axis=1, tiled=True),
    )
    joined = jnp.concatenate(
        [
            query_back.reshape(frames * records, features),
            key_backward.reshape(frames * records, features),
            value_back.reshape(frames * records, features),
        ],
        axis=1,
    )
    norm_grad = lax.dot_general(
        joined,
        lax.all_gather(qkv_weight[0], "seq", axis=0, tiled=True),
        ROW_DOT,
        preferred_element_type=jnp.float32,
    )
    inputs = layer_input[0].reshape(frames * records, model_width).astype(jnp.float32)
    row_average = jnp.mean(inputs, axis=1, keepdims=True)
    centered_input = inputs - row_average
    var = jnp.mean(centered_input * centered_input, axis=1, keepdims=True)
    inverse_deviation = 1.0 / jnp.sqrt(var + EPSILON)
    normalized_input = centered_input * inverse_deviation
    scaled_rows = norm_grad * norm_gain[0][None, :]
    residual_branch = inverse_deviation * (
        scaled_rows
        - jnp.mean(scaled_rows, axis=1, keepdims=True)
        - normalized_input * jnp.mean(scaled_rows * normalized_input, axis=1, keepdims=True)
    )
    input_grad = (flat_grad.astype(jnp.float32) + residual_branch).astype(jnp.bfloat16)
    input_grad = input_grad.reshape(1, frames, records, model_width)
    return shifted(input_grad, "section", -1)


def body(
    dims,
    length_ref,
    li_ref,
    q_ref,
    k_ref,
    v_ref,
    og_ref,
    ow_in,
    w_in,
    gain_ref,
    out_ref,
    xq,
    xk,
    xv,
    xo,
    g,
    ow,
    ow_via,
    w,
    joined,
    part_send,
    side_recv,
    sum_send,
    part_recv,
    li_here,
    og_here,
    lens,
    gains,
    x_send_sem,
    x_recv_sem,
    o_send_sem,
    o_pass_sem,
    o_recv_sem,
    ow_send_sem,
    ow_pass_sem,
    ow_recv_sem,
    via_send_sem,
    via_recv_sem,
    w_send_sem,
    w_pass_sem,
    w_recv_sem,
    side_send_sem,
    side_recv_sem,
    p_send_sem,
    p_recv_sem,
    s_send_sem,
    s_recv_sem,
    twin_send_sem,
    twin_recv_sem,
):
    n, sections, records, parts, frames, cols = dims
    pairs = cols // (2 * HS)
    section = lax.axis_index("section")
    me = lax.axis_index("seq")
    core = section % 2
    z = me // parts
    part = me % parts
    half = z // 2
    twin = section + 1 - 2 * core
    work = section - core + half
    record = 2 * (z % 2) + core
    lead = core == half
    near = z == 1 + half
    prior = (section + sections - 1) % sections
    before = (work + sections - 1) % sections

    def remote(src, dst, send, recv, sec, dev):
        return pltpu.make_async_remote_copy(
            src_ref=src,
            dst_ref=dst,
            send_sem=send,
            recv_sem=recv,
            device_id=(sec, dev),
            device_id_type=pl.DeviceIdType.MESH,
        )

    def either(stays, copy_here, copy_there):
        @pl.when(stays)
        def _():
            copy_here().start()

        @pl.when(jnp.logical_not(stays))
        def _():
            copy_there().start()

    barrier = pltpu.get_barrier_semaphore()
    for s in range(sections):
        for k in range(n):
            if s or k:
                pl.semaphore_signal(
                    barrier,
                    inc=1,
                    device_id=((section + s) % sections, (me + k) % n),
                    device_id_type=pl.DeviceIdType.MESH,
                )

    lane = lax.broadcasted_iota(jnp.int32, lens.shape[1:], 1)
    lengths = jnp.zeros(lens.shape[1:], jnp.int32)
    for r in range(records):
        lengths = jnp.where(lane == r, length_ref[r], lengths)
    lens[0] = lengths

    pl.semaphore_wait(barrier, sections * n - 1)

    twin_lens = remote(lens.at[0], lens.at[1], twin_send_sem.at[0], twin_recv_sem.at[0], twin, me)
    twin_gain = remote(gain_ref, gains, twin_send_sem.at[1], twin_recv_sem.at[1], twin, me)

    def seat(r, p):
        return section - core + r % 2, (2 * core + r // 2) * parts + p

    def turn(i):
        return (i + 2 * core) % records

    heads = [(q_ref, xq), (k_ref, xk), (v_ref, xv)]

    def x_source(t, r, p):
        return heads[t][0].at[r, :, pl.ds(p * cols, cols)]

    def x_copy(t, i, p):
        r = turn(i)
        sec, dev = seat(r, p)
        return remote(
            x_source(t, r, p),
            heads[t][1].at[me],
            x_send_sem.at[t, i, p],
            x_recv_sem.at[t, me],
            sec,
            dev,
        )

    def x_stays(i, p):
        return lead & (turn(i) == record) & (part == p)

    def x_start(t):
        for i in range(records):
            for p in range(parts):
                either(
                    x_stays(i, p),
                    lambda: pltpu.make_async_copy(
                        x_source(t, turn(i), p), heads[t][1].at[me], x_recv_sem.at[t, me]
                    ),
                    lambda: x_copy(t, i, p),
                )

    def og_source(r):
        return og_ref.at[pl.ds(pl.multiple_of(r * frames, frames), frames)]

    def o_copy(i):
        r = turn(i)
        sec, dev = seat(r, part)
        return remote(og_source(r), xo.at[me], o_send_sem.at[i], o_recv_sem.at[me], sec, dev)

    def o_stays(i):
        return lead & (turn(i) == record)

    def o_pass(k):
        slot = k * parts + part
        return remote(
            xo.at[slot],
            xo.at[slot],
            o_pass_sem.at[k],
            o_recv_sem.at[slot],
            section,
            z * parts + 1 - part,
        )

    def lead_z(d):
        return 1 + core if d == 0 else 3 * core

    ow_slot = me % records

    def ow_copy(d):
        return remote(
            ow_in,
            ow.at[ow_slot],
            ow_send_sem.at[d],
            ow_recv_sem.at[ow_slot],
            section,
            lead_z(d) * parts + half,
        )

    through = part != half

    def via_copy():
        return remote(
            ow_in,
            ow_via.at[z % 2],
            via_send_sem.at[0, 0],
            via_recv_sem.at[z % 2],
            section,
            (1 + core) * parts + part,
        )

    def via_on(k, way):
        slot = k * parts + part
        dev = (1 + half if way == 0 else 3 * half) * parts + 1 - half
        return remote(
            ow_via.at[k],
            ow.at[slot],
            via_send_sem.at[1 + way, k],
            ow_recv_sem.at[slot],
            section,
            dev,
        )

    def near_copy():
        return remote(
            ow_in,
            ow.at[ow_slot],
            ow_send_sem.at[0],
            ow_recv_sem.at[ow_slot],
            section,
            (1 + core) * parts + part,
        )

    def ow_stays(d):
        return (lead_z(d) == z) & (part == half)

    def w_source(t, p):
        return w_in.at[:, pl.ds(pl.multiple_of((t * parts + p) * cols, cols), cols)]

    def w_target(t):
        return w.at[me, :, pl.ds(t * cols, cols)]

    def w_copy(d, p, t):
        return remote(
            w_source(t, p),
            w_target(t),
            w_send_sem.at[d, p, t],
            w_recv_sem.at[me, t],
            section,
            lead_z(d) * parts + p,
        )

    def w_stays(d, p):
        return (lead_z(d) == z) & (part == p)

    def sends(d):
        return lead | (d == 0)

    def ow_start(d):
        either(
            ow_stays(d),
            lambda: pltpu.make_async_copy(ow_in, ow.at[ow_slot], ow_recv_sem.at[ow_slot]),
            lambda: ow_copy(d),
        )

    def w_start(t, d, p):
        either(
            w_stays(d, p),
            lambda: pltpu.make_async_copy(w_source(t, p), w_target(t), w_recv_sem.at[me, t]),
            lambda: w_copy(d, p, t),
        )

    def w_starts(t):
        for q in range(parts):
            p = (part + q) % parts
            w_start(t, 0, p)

            @pl.when(lead)
            def _():
                w_start(t, 1, p)

    def ow_on(slot, way):
        sec, dev = (twin, me) if way == 0 else (section, 3 * half * parts + part)
        return remote(
            ow.at[slot], ow.at[slot], ow_pass_sem.at[way, slot], ow_recv_sem.at[slot], sec, dev
        )

    def w_on(slot, t, way):
        sec, dev = (twin, me) if way == 0 else (section, 3 * half * parts + part)
        at = w.at[slot, :, pl.ds(t * cols, cols)]
        return remote(at, at, w_pass_sem.at[way, slot, t], w_recv_sem.at[slot, t], sec, dev)

    relays = lead & near
    ow_relays = relays & (part != half)
    via_relays = relays & (part == half)

    def w_relays(origin):
        return lead & near & (origin // 2 != half)

    def w_pass(origin, t):
        for q in range(parts):
            slot = origin * parts + (part + q) % parts
            w_on(slot, t, 0).wait_recv()

            @pl.when(w_relays(origin))
            def _():
                w_on(slot, t, 1).start()

            @pl.when(lead)
            def _():
                w_on(slot, t, 0).start()

    def order(i):
        return (z, 2 * half + 1 - z % 2, 2 - half, 3 - 3 * half)[i]

    shift_og = remote(og_ref, og_here, s_send_sem.at[0], s_recv_sem.at[0], prior, me)
    shift_li = remote(li_ref, li_here, s_send_sem.at[1], s_recv_sem.at[1], prior, me)

    twin_lens.start()
    twin_gain.start()
    @pl.when(lead)
    def _():
        ow_start(0)
        ow_start(1)

    @pl.when(jnp.logical_not(lead))
    def _():
        @pl.when(part == half)
        def _():
            near_copy().start()

        @pl.when(part != half)
        def _():
            via_copy().start()

    for i in range(records):
        r = turn(i)
        either(
            o_stays(i),
            lambda: pltpu.make_async_copy(og_source(r), xo.at[me], o_recv_sem.at[me]),
            lambda: o_copy(i),
        )
    for t in range(3):
        x_start(t)
    for t in range(3):
        w_starts(t)
    shift_og.start()
    shift_li.start()

    @pl.when(via_relays)
    def _():
        for k in range(2):
            remote(
                ow_via.at[k],
                ow_via.at[k],
                via_send_sem.at[0, k],
                via_recv_sem.at[k],
                section,
                me,
            ).wait_recv()
            via_on(k, 1).start()
            via_on(k, 0).start()

    for slot in range(records):
        ow_on(slot, 0).wait_recv()
        if slot % parts == 0:

            @pl.when(ow_relays & (part == 0))
            def _():
                ow_on(slot, 1).start()
        else:

            @pl.when(ow_relays & (part == 1))
            def _():
                ow_on(slot, 1).start()

        @pl.when(lead)
        def _():
            ow_on(slot, 0).start()

    for k in range(records):
        o_pass(k).wait_recv()
        o_pass(k).start()
    for k in range(records):
        slot = k * parts + 1 - part
        remote(
            xo.at[slot], xo.at[slot], o_pass_sem.at[k], o_recv_sem.at[slot], section, me
        ).wait_recv()

    length = n * frames
    rows_here = ow.shape[1]

    def project(i, carry):
        weight = ow[pl.ds(2 * i, 2)].reshape(2 * rows_here, ow.shape[2])
        grads = xo[...].reshape(length, xo.shape[2])
        lanes = pl.ds(pl.multiple_of(i * 2 * rows_here, 2 * rows_here), 2 * rows_here)
        g[:, lanes] = lax.dot_general(
            grads, weight, ROW_DOT, preferred_element_type=jnp.float32
        ).astype(jnp.bfloat16)
        return carry

    lax.fori_loop(0, cols // (2 * rows_here), project, 0)
    twin_lens.wait_recv()
    twin_gain.wait_recv()
    for t in range(3):
        for j in range(n):
            remote(
                heads[t][1].at[j],
                heads[t][1].at[j],
                x_send_sem.at[t, 0, 0],
                x_recv_sem.at[t, j],
                section,
                me,
            ).wait_recv()

    valid = jnp.where(lead, lens[0], lens[1])
    valid = jnp.sum(jnp.where(lane == record, valid, 0), axis=1, keepdims=True)[:1]
    keys_ok = lax.broadcasted_iota(jnp.int32, (length, 1), 0) < valid
    low_lanes = lax.broadcasted_iota(jnp.int32, (length, 2 * HS), 1) < HS
    scale = HS ** (-0.5)

    plan = [(0, 0, 0), (0, 0, 1), (0, 0, 2), (1, 1, 0), (1, 1, 1), (1, 1, 2)]
    plan += [(3, 2, 0), (3, 3, 0), (6, 2, 1), (6, 3, 1)]
    steps = 2 * pairs

    def between(step):
        for at in sorted({s for s, _, _ in plan}):

            @pl.when(step == min(at, steps - 1))
            def _():
                for s, i, t in plan:
                    if s == at:
                        w_pass(order(i), t)

    def attend(j, carry):
        lanes = pl.ds(pl.multiple_of(j * 2 * HS, 2 * HS), 2 * HS)
        queries, keys, values = (x[:, :, lanes].reshape(length, 2 * HS) for x in (xq, xk, xv))
        grads = g[:, lanes]
        keys_across = keys.T
        nothing = jnp.zeros_like(keys)
        halves = []
        for h in range(2):
            mine = low_lanes if h == 0 else jnp.logical_not(low_lanes)
            key_h = jnp.where(mine, keys, nothing)
            value_h = jnp.where(mine, values, nothing)
            scores = (
                lax.dot_general(key_h, queries, ROW_DOT, preferred_element_type=jnp.float32)
                * scale
            )
            scores = jnp.where(keys_ok, scores, MASKED)
            weights = jnp.exp(scores - jnp.max(scores, axis=0, keepdims=True))
            probs = weights * (1.0 / jnp.sum(weights, axis=0, keepdims=True))
            grad_probs = lax.dot_general(
                value_h, grads, ROW_DOT, preferred_element_type=jnp.float32
            )
            centre = jnp.sum(probs * grad_probs, axis=0, keepdims=True)
            grad_scores = (probs * (grad_probs - centre)).astype(jnp.bfloat16)
            value_grad = jnp.dot(
                probs.astype(jnp.bfloat16), grads, preferred_element_type=jnp.float32
            )
            key_grad = jnp.dot(grad_scores, queries, preferred_element_type=jnp.float32)
            query_grad = jnp.dot(
                keys_across[h * HS : (h + 1) * HS], grad_scores, preferred_element_type=jnp.float32
            )
            halves.append((query_grad, key_grad, value_grad))
            between(2 * j + h)
        (query_0, key_0, value_0), (query_1, key_1, value_1) = halves
        query_both = (jnp.concatenate([query_0, query_1], axis=0) * scale).T
        key_both = jnp.where(low_lanes, key_0, key_1) * scale
        value_both = jnp.where(low_lanes, value_0, value_1)
        for t, both in enumerate((query_both, key_both, value_both)):
            at = pl.multiple_of(t * cols + j * 2 * HS, 2 * HS)
            joined[:, pl.ds(at, 2 * HS)] = both.astype(jnp.bfloat16)

        return carry

    lax.fori_loop(0, pairs, attend, 0)

    def side_copy(origin):
        other = 1 - part
        return remote(
            part_send.at[origin, other],
            side_recv.at[origin],
            side_send_sem.at[origin],
            side_recv_sem.at[origin],
            section,
            z * parts + other,
        )

    def sum_copy(origin, to):
        return remote(
            sum_send.at[origin, to],
            part_recv.at[record, origin],
            p_send_sem.at[origin, to],
            p_recv_sem.at[record, origin],
            before,
            to * parts + part,
        )

    def sum_stays(to):
        return (before == section) & (to == z)

    def norm_block(origin):
        weight = w[pl.ds(origin * parts, parts)].reshape(parts * w.shape[1], w.shape[2])
        sums = lax.dot_general(
            joined[...], weight, ROW_DOT, preferred_element_type=jnp.float32
        )
        gain = jnp.where(lead, gain_ref[origin], gains[origin])
        sums = (sums * gain).astype(jnp.bfloat16)
        sums = sums.reshape(records, parts, frames, sums.shape[1])
        for other in range(parts):
            part_send[origin, other] = sums[:, other]
        side_copy(origin).start()

    def norm_send(origin):
        side_copy(origin).wait_recv()
        total = part_send[origin, part].astype(jnp.float32)
        total = total + side_recv[origin].astype(jnp.float32)
        sum_send[origin] = total.astype(jnp.bfloat16)
        for k in range(records):
            to = (z + k) % records
            either(
                sum_stays(to),
                lambda: pltpu.make_async_copy(
                    sum_send.at[origin, to],
                    part_recv.at[record, origin],
                    p_recv_sem.at[record, origin],
                ),
                lambda: sum_copy(origin, to),
            )

    def norm(i, carry):
        origin = jnp.where(
            i == 0, order(0), jnp.where(i == 1, order(1), jnp.where(i == 2, order(2), order(3)))
        )
        last = jnp.where(i == 1, order(0), jnp.where(i == 2, order(1), order(2)))

        @pl.when(i == 2)
        def _():
            norm_send(last)
            w_pass(order(2), 2)
            w_pass(order(3), 2)

        norm_block(origin)

        @pl.when((i == 1) | (i == records - 1))
        def _():
            norm_send(last)

        @pl.when(i == records - 1)
        def _():
            norm_send(origin)

        return carry

    lax.fori_loop(0, records, norm, 0)

    shift_og.wait_recv()
    shift_li.wait_recv()
    for src in range(records):
        for origin in range(records):
            remote(
                sum_send.at[origin, 0],
                part_recv.at[src, origin],
                p_send_sem.at[origin, 0],
                p_recv_sem.at[src, origin],
                before,
                me,
            ).wait_recv()

    width = og_here.shape[1]

    def finish(r):
        rows = pl.ds(r * frames, frames)
        inputs = li_here[:, r, :].astype(jnp.float32)
        centered = inputs - jnp.sum(inputs, axis=1, keepdims=True) * (1.0 / width)
        var = jnp.sum(centered * centered, axis=1, keepdims=True) * (1.0 / width)
        deviation = 1.0 / jnp.sqrt(var + EPSILON)
        normal = centered * deviation
        scaled = []
        for origin in range(records):
            scaled.append(part_recv[r, origin].astype(jnp.float32))
        scaled = jnp.concatenate(scaled, axis=1)
        average = jnp.sum(scaled, axis=1, keepdims=True) * (1.0 / width)
        along = jnp.sum(scaled * normal, axis=1, keepdims=True) * (1.0 / width)
        branch = deviation * (scaled - average - normal * along)
        out_ref[rows, :] = (og_here[rows, :].astype(jnp.float32) + branch).astype(jnp.bfloat16)

    for r in range(records):
        finish(r)

    def sent(stays, copy):
        @pl.when(jnp.logical_not(stays))
        def _():
            copy.wait_send()

    twin_lens.wait_send()
    twin_gain.wait_send()
    shift_og.wait_send()
    shift_li.wait_send()
    for i in range(records):
        sent(o_stays(i), o_copy(i))
        o_pass(i).wait_send()
        for t in range(3):
            for p in range(parts):
                sent(x_stays(i, p), x_copy(t, i, p))
    for d in range(2):

        @pl.when(sends(d))
        def _():
            for p in range(parts):
                for t in range(3):
                    sent(w_stays(d, p), w_copy(d, p, t))

        @pl.when(lead)
        def _():
            sent(ow_stays(d), ow_copy(d))

    @pl.when(jnp.logical_not(lead) & (part == half))
    def _():
        near_copy().wait_send()

    @pl.when(jnp.logical_not(lead) & (part != half))
    def _():
        via_copy().wait_send()

    @pl.when(via_relays)
    def _():
        for k in range(2):
            via_on(k, 1).wait_send()
            via_on(k, 0).wait_send()

    for slot in range(records):

        @pl.when(ow_relays & (part == slot % parts))
        def _():
            ow_on(slot, 1).wait_send()

    @pl.when(lead)
    def _():
        for slot in range(records):
            ow_on(slot, 0).wait_send()
        for slot in range(n):
            for t in range(3):
                w_on(slot, t, 0).wait_send()

    for origin in range(records):

        @pl.when(w_relays(origin))
        def _():
            for other in range(parts):
                for t in range(3):
                    w_on(origin * parts + other, t, 1).wait_send()

        side_copy(origin).wait_send()
        for to in range(records):
            sent(sum_stays(to), sum_copy(origin, to))


def on_device_fused(
    layer_input,
    norm_gain,
    queries,
    key_states,
    value_states,
    out_grad,
    out_weight,
    qkv_weight,
    lengths,
):
    n = lax.axis_size("seq")
    sections = lax.axis_size("section")
    frames, records, features = queries.shape[1:]
    width = out_grad.shape[3]
    parts = n // records
    cols = features // parts
    ow_rows = out_weight.shape[1]
    w_rows = qkv_weight.shape[1]
    block = parts * w_rows

    def by_record(x):
        return x[0].transpose(1, 0, 2)

    flat_grad = by_record(out_grad).reshape(records * frames, width)
    gain = norm_gain[0].reshape(records, 1, block)
    vmem = pl.BlockSpec(memory_space=pltpu.VMEM)
    low = jnp.bfloat16
    dma = pltpu.SemaphoreType.DMA
    out = pl.pallas_call(
        functools.partial(body, (n, sections, records, parts, frames, cols)),
        out_shape=jax.ShapeDtypeStruct((records * frames, width), low),
        in_specs=[pl.BlockSpec(memory_space=pltpu.SMEM)] + [vmem] * 8,
        out_specs=vmem,
        scratch_shapes=[pltpu.VMEM((n, frames, cols), low)] * 3
        + [
            pltpu.VMEM((n, frames, width), low),
            pltpu.VMEM((n * frames, cols), low),
            pltpu.VMEM((records, ow_rows, width), low),
            pltpu.VMEM((2, ow_rows, width), low),
            pltpu.VMEM((n, w_rows, 3 * cols), low),
            pltpu.VMEM((n * frames, 3 * cols), low),
            pltpu.VMEM((records, parts, records, frames, block), low),
            pltpu.VMEM((records, records, frames, block), low),
            pltpu.VMEM((records, records, frames, block), low),
            pltpu.VMEM((records, records, frames, block), low),
            pltpu.VMEM((frames, records, width), low),
            pltpu.VMEM((records * frames, width), low),
            pltpu.VMEM((2, 8, 128), jnp.int32),
            pltpu.VMEM((records, 1, block), jnp.float32),
            dma((3, records, parts)),
            dma((3, n)),
            dma((records,)),
            dma((records,)),
            dma((n,)),
            dma((2,)),
            dma((2, records)),
            dma((records,)),
            dma((3, 2)),
            dma((2,)),
            dma((2, parts, 3)),
            dma((2, n, 3)),
            dma((n, 3)),
            dma((records,)),
            dma((records,)),
            dma((records, records)),
            dma((records, records)),
            dma((2,)),
            dma((2,)),
            dma((2,)),
            dma((2,)),
        ],
        compiler_params=pltpu.CompilerParams(
            collective_id=0, has_side_effects=True, vmem_limit_bytes=60 * 1024 * 1024
        ),
    )(
        lengths[0],
        layer_input[0],
        by_record(queries),
        by_record(key_states),
        by_record(value_states),
        flat_grad,
        out_weight[0],
        qkv_weight[0],
        gain,
    )
    return out.reshape(records, frames, width).transpose(1, 0, 2)[None]


def fits(mesh, records, features):
    n = mesh.shape["seq"]
    if n != 2 * records or records != 4 or mesh.shape["section"] % 2:
        return False
    return features % (n * HS) == 0


def solution(mesh):
    in_specs = (
        P("section", "seq", None, None),
        P("section", None),
        P("section", "seq", None, None),
        P("section", "seq", None, None),
        P("section", "seq", None, None),
        P("section", "seq", None, None),
        P("section", "seq", None),
        P("section", "seq", None),
        P("section", None),
    )
    out_specs = P("section", "seq", None, None)

    def run(*arrays):
        fused = fits(mesh, arrays[2].shape[2], arrays[2].shape[3])
        return jax.shard_map(
            on_device_fused if fused else on_device,
            mesh=mesh,
            in_specs=in_specs,
            out_specs=out_specs,
            check_vma=False,
        )(*arrays)

    return run
```

```python
import functools

import jax
import jax.numpy as jnp
from jax import lax
from jax.experimental import pallas as pl
from jax.experimental.pallas import tpu as pltpu
from jax.sharding import PartitionSpec as P

HEADS = 16
HS = 64


EPSILON = 1e-05
MASKED = -1e30
ROW_DOT = (((1,), (1,)), ((), ()))
COL_DOT = (((0,), (0,)), ((), ()))


def shifted(shard, axis, by):
    count = lax.axis_size(axis)
    return lax.ppermute(shard, axis, [(i, (i + by) % count) for i in range(count)])


def item_backward(query_rows, key_rows, value_rows, grad_rows, key_valid):
    length = query_rows.shape[0]
    block = min(512, length)
    scale = HS ** (-0.5)
    offsets = jnp.arange(0, length, block)
    zeros = jnp.zeros((length, query_rows.shape[1]), jnp.float32)

    def step(carry, offset):
        key_total, value_total = carry
        query_block = lax.dynamic_slice_in_dim(query_rows, offset, block, 0)
        grad_block = lax.dynamic_slice_in_dim(grad_rows, offset, block, 0)
        scores = (
            lax.dot_general(query_block, key_rows, ROW_DOT, preferred_element_type=jnp.float32)
            * scale
        )
        scores = jnp.where(key_valid[None, :], scores, MASKED)
        largest = jnp.max(scores, axis=1, keepdims=True)
        weights = jnp.exp(scores - largest)
        probs = weights / jnp.sum(weights, axis=1, keepdims=True)
        probs_low = probs.astype(jnp.bfloat16)
        grad_probs = lax.dot_general(
            grad_block, value_rows, ROW_DOT, preferred_element_type=jnp.float32
        )
        centre = jnp.sum(probs * grad_probs, axis=1, keepdims=True)
        grad_scores = (probs * (grad_probs - centre) * scale).astype(jnp.bfloat16)
        query_grad = jnp.dot(grad_scores, key_rows, preferred_element_type=jnp.float32)
        key_total = key_total + lax.dot_general(
            grad_scores, query_block, COL_DOT, preferred_element_type=jnp.float32
        )
        value_total = value_total + lax.dot_general(
            probs_low, grad_block, COL_DOT, preferred_element_type=jnp.float32
        )
        return ((key_total, value_total), query_grad.astype(jnp.bfloat16))

    (key_total, value_total), query_parts = lax.scan(step, (zeros, zeros), offsets)
    query_grad = query_parts.reshape(length, query_rows.shape[1])
    return (query_grad, key_total.astype(jnp.bfloat16), value_total.astype(jnp.bfloat16))


def split_items(columns):
    length = columns.shape[0]
    count = columns.shape[1] // HS
    return columns.reshape(length, count, HS).transpose(1, 0, 2)


def join_items(items):
    count = items.shape[0]
    length = items.shape[1]
    return items.transpose(1, 0, 2).reshape(length, count * HS)


def project_grad(flat_grad, out_rows):
    return lax.dot_general(
        flat_grad,
        lax.all_gather(out_rows, "seq", axis=0, tiled=True),
        ROW_DOT,
        preferred_element_type=jnp.float32,
    ).astype(jnp.bfloat16)


def on_device(
    layer_input,
    norm_gain,
    queries,
    key_states,
    value_states,
    out_grad,
    out_weight,
    qkv_weight,
    lengths,
):
    frames = queries.shape[1]
    records = queries.shape[2]
    features = queries.shape[3]
    model_width = out_grad.shape[3]
    flat_grad = out_grad[0].reshape(frames * records, model_width)
    frame_queries = queries[0].reshape(frames, records * features)
    frame_keys = key_states[0].reshape(frames, records * features)
    frame_values = value_states[0].reshape(frames, records * features)
    attn_grad = project_grad(flat_grad, out_weight[0])
    head_queries, head_keys, head_values, head_grads = (
        lax.all_to_all(frame_queries, "seq", split_axis=1, concat_axis=0, tiled=True),
        lax.all_to_all(frame_keys, "seq", split_axis=1, concat_axis=0, tiled=True),
        lax.all_to_all(frame_values, "seq", split_axis=1, concat_axis=0, tiled=True),
        lax.all_to_all(
            attn_grad.reshape(frames, records * features),
            "seq",
            split_axis=1,
            concat_axis=0,
            tiled=True,
        ),
    )
    items_here = head_queries.shape[1] // HS
    length = head_queries.shape[0]
    item_ids = lax.axis_index("seq") * items_here + jnp.arange(items_here, dtype=jnp.int32)
    record_ids = item_ids // HEADS
    record_pick = jnp.arange(records, dtype=jnp.int32)[None, :] == record_ids[:, None]
    item_lengths = jnp.sum(jnp.where(record_pick, lengths[0][None, :], 0), axis=1)
    key_valid = jnp.arange(length, dtype=jnp.int32)[None, :] < item_lengths[:, None]
    query_grad, key_gradient, value_grad = lax.map(
        lambda group: item_backward(*group),
        (
            split_items(head_queries),
            split_items(head_keys),
            split_items(head_values),
            split_items(head_grads),
            key_valid,
        ),
    )
    query_back, key_backward, value_back = (
        lax.all_to_all(join_items(query_grad), "seq", split_axis=0, concat_axis=1, tiled=True),
        lax.all_to_all(join_items(key_gradient), "seq", split_axis=0, concat_axis=1, tiled=True),
        lax.all_to_all(join_items(value_grad), "seq", split_axis=0, concat_axis=1, tiled=True),
    )
    joined = jnp.concatenate(
        [
            query_back.reshape(frames * records, features),
            key_backward.reshape(frames * records, features),
            value_back.reshape(frames * records, features),
        ],
        axis=1,
    )
    norm_grad = lax.dot_general(
        joined,
        lax.all_gather(qkv_weight[0], "seq", axis=0, tiled=True),
        ROW_DOT,
        preferred_element_type=jnp.float32,
    )
    inputs = layer_input[0].reshape(frames * records, model_width).astype(jnp.float32)
    row_average = jnp.mean(inputs, axis=1, keepdims=True)
    centered_input = inputs - row_average
    var = jnp.mean(centered_input * centered_input, axis=1, keepdims=True)
    inverse_deviation = 1.0 / jnp.sqrt(var + EPSILON)
    normalized_input = centered_input * inverse_deviation
    scaled_rows = norm_grad * norm_gain[0][None, :]
    residual_branch = inverse_deviation * (
        scaled_rows
        - jnp.mean(scaled_rows, axis=1, keepdims=True)
        - normalized_input * jnp.mean(scaled_rows * normalized_input, axis=1, keepdims=True)
    )
    input_grad = (flat_grad.astype(jnp.float32) + residual_branch).astype(jnp.bfloat16)
    input_grad = input_grad.reshape(1, frames, records, model_width)
    return shifted(input_grad, "section", -1)


def body(
    dims,
    length_ref,
    li_ref,
    q_in,
    k_in,
    v_in,
    og_in,
    ow_in,
    w_in,
    gain_ref,
    out_ref,
    q_ref,
    k_ref,
    v_ref,
    og_ref,
    xq,
    xk,
    xv,
    xo,
    g,
    ow,
    ow_via,
    w,
    joined,
    part_send,
    side_recv,
    sum_send,
    part_recv,
    li_here,
    og_here,
    normals,
    deviations,
    lens,
    gains,
    x_send_sem,
    x_recv_sem,
    o_send_sem,
    o_pass_sem,
    o_recv_sem,
    ow_send_sem,
    ow_pass_sem,
    ow_recv_sem,
    via_send_sem,
    via_recv_sem,
    w_send_sem,
    w_pass_sem,
    w_recv_sem,
    side_send_sem,
    side_recv_sem,
    p_send_sem,
    p_recv_sem,
    s_send_sem,
    s_recv_sem,
    twin_send_sem,
    twin_recv_sem,
):
    n, sections, records, parts, frames, cols = dims
    pairs = cols // (2 * HS)
    section = lax.axis_index("section")
    me = lax.axis_index("seq")
    core = section % 2
    z = me // parts
    part = me % parts
    half = z // 2
    twin = section + 1 - 2 * core
    work = section - core + half
    record = 2 * (z % 2) + core
    lead = core == half
    near = z == 1 + half
    prior = (section + sections - 1) % sections
    before = (work + sections - 1) % sections

    def remote(src, dst, send, recv, sec, dev):
        return pltpu.make_async_remote_copy(
            src_ref=src,
            dst_ref=dst,
            send_sem=send,
            recv_sem=recv,
            device_id=(sec, dev),
            device_id_type=pl.DeviceIdType.MESH,
        )

    def either(stays, copy_here, copy_there):
        @pl.when(stays)
        def _():
            copy_here().start()

        @pl.when(jnp.logical_not(stays))
        def _():
            copy_there().start()

    barrier = pltpu.get_barrier_semaphore()
    for s in range(sections):
        for k in range(n):
            if s or k:
                pl.semaphore_signal(
                    barrier,
                    inc=1,
                    device_id=((section + s) % sections, (me + k) % n),
                    device_id_type=pl.DeviceIdType.MESH,
                )

    lane = lax.broadcasted_iota(jnp.int32, lens.shape[1:], 1)
    lengths = jnp.zeros(lens.shape[1:], jnp.int32)
    for r in range(records):
        lengths = jnp.where(lane == r, length_ref[r], lengths)
    lens[0] = lengths

    def by_record(source, target):
        for r in range(records):
            if len(target.shape) == 2:
                target[r * frames : (r + 1) * frames] = source[:, r, :]
            else:
                target[r] = source[:, r, :]

    by_record(og_in, og_ref)
    pl.semaphore_wait(barrier, sections * n - 1)

    twin_lens = remote(lens.at[0], lens.at[1], twin_send_sem.at[0], twin_recv_sem.at[0], twin, me)
    twin_gain = remote(gain_ref, gains, twin_send_sem.at[1], twin_recv_sem.at[1], twin, me)

    def seat(r, p):
        return section - core + r % 2, (2 * core + r // 2) * parts + p

    def turn(i):
        return (i + 2 * core) % records

    heads = [(q_ref, xq), (k_ref, xk), (v_ref, xv)]

    def x_source(t, r, p):
        return heads[t][0].at[r, :, pl.ds(p * cols, cols)]

    def x_copy(t, i, p):
        r = turn(i)
        sec, dev = seat(r, p)
        return remote(
            x_source(t, r, p),
            heads[t][1].at[me],
            x_send_sem.at[t, i, p],
            x_recv_sem.at[t, me],
            sec,
            dev,
        )

    def x_stays(i, p):
        return lead & (turn(i) == record) & (part == p)

    def x_start(t):
        for i in range(records):
            for p in range(parts):
                either(
                    x_stays(i, p),
                    lambda: pltpu.make_async_copy(
                        x_source(t, turn(i), p), heads[t][1].at[me], x_recv_sem.at[t, me]
                    ),
                    lambda: x_copy(t, i, p),
                )

    def og_source(r):
        return og_ref.at[pl.ds(pl.multiple_of(r * frames, frames), frames)]

    def o_copy(i):
        r = turn(i)
        sec, dev = seat(r, part)
        return remote(og_source(r), xo.at[me], o_send_sem.at[i], o_recv_sem.at[me], sec, dev)

    def o_stays(i):
        return lead & (turn(i) == record)

    def o_pass(k):
        slot = k * parts + part
        return remote(
            xo.at[slot],
            xo.at[slot],
            o_pass_sem.at[k],
            o_recv_sem.at[slot],
            section,
            z * parts + 1 - part,
        )

    def lead_z(d):
        return 1 + core if d == 0 else 3 * core

    ow_slot = me % records

    def ow_copy(d):
        return remote(
            ow_in,
            ow.at[ow_slot],
            ow_send_sem.at[d],
            ow_recv_sem.at[ow_slot],
            section,
            lead_z(d) * parts + half,
        )

    through = part != half

    def via_copy():
        return remote(
            ow_in,
            ow_via.at[z % 2],
            via_send_sem.at[0, 0],
            via_recv_sem.at[z % 2],
            section,
            (1 + core) * parts + part,
        )

    def via_on(k, way):
        slot = k * parts + part
        dev = (1 + half if way == 0 else 3 * half) * parts + 1 - half
        return remote(
            ow_via.at[k],
            ow.at[slot],
            via_send_sem.at[1 + way, k],
            ow_recv_sem.at[slot],
            section,
            dev,
        )

    def near_copy():
        return remote(
            ow_in,
            ow.at[ow_slot],
            ow_send_sem.at[0],
            ow_recv_sem.at[ow_slot],
            section,
            (1 + core) * parts + part,
        )

    def ow_stays(d):
        return (lead_z(d) == z) & (part == half)

    def w_source(t, p):
        return w_in.at[:, pl.ds(pl.multiple_of((t * parts + p) * cols, cols), cols)]

    def w_target(t):
        return w.at[me, :, pl.ds(t * cols, cols)]

    def w_copy(d, p, t):
        return remote(
            w_source(t, p),
            w_target(t),
            w_send_sem.at[d, p, t],
            w_recv_sem.at[me, t],
            section,
            lead_z(d) * parts + p,
        )

    def w_stays(d, p):
        return (lead_z(d) == z) & (part == p)

    def sends(d):
        return lead | (d == 0)

    def ow_start(d):
        either(
            ow_stays(d),
            lambda: pltpu.make_async_copy(ow_in, ow.at[ow_slot], ow_recv_sem.at[ow_slot]),
            lambda: ow_copy(d),
        )

    def w_start(t, d, p):
        either(
            w_stays(d, p),
            lambda: pltpu.make_async_copy(w_source(t, p), w_target(t), w_recv_sem.at[me, t]),
            lambda: w_copy(d, p, t),
        )

    def w_starts(t, d):
        for q in range(parts):
            p = (part + q) % parts
            w_start(t, d, p)

    def ow_on(slot, way):
        sec, dev = (twin, me) if way == 0 else (section, 3 * half * parts + part)
        return remote(
            ow.at[slot], ow.at[slot], ow_pass_sem.at[way, slot], ow_recv_sem.at[slot], sec, dev
        )

    def w_on(slot, t, way):
        sec, dev = (twin, me) if way == 0 else (section, 3 * half * parts + part)
        at = w.at[slot, :, pl.ds(t * cols, cols)]
        return remote(at, at, w_pass_sem.at[way, slot, t], w_recv_sem.at[slot, t], sec, dev)

    relays = lead & near
    ow_relays = relays & (part != half)
    via_relays = relays & (part == half)

    def w_relays(origin):
        return lead & near & (origin // 2 != half)

    def w_pass(origin, t):
        for q in range(parts):
            slot = origin * parts + (part + q) % parts
            w_on(slot, t, 0).wait_recv()

            @pl.when(w_relays(origin))
            def _():
                w_on(slot, t, 1).start()

            @pl.when(lead)
            def _():
                w_on(slot, t, 0).start()

    def order(i):
        return (z, 2 * half + 1 - z % 2, 2 - half, 3 - 3 * half)[i]

    shift_og = remote(og_ref, og_here, s_send_sem.at[0], s_recv_sem.at[0], prior, me)
    shift_li = remote(li_ref, li_here, s_send_sem.at[1], s_recv_sem.at[1], prior, me)

    twin_lens.start()
    twin_gain.start()
    @pl.when(lead)
    def _():
        ow_start(0)
        ow_start(1)

    @pl.when(jnp.logical_not(lead))
    def _():
        @pl.when(part == half)
        def _():
            near_copy().start()

        @pl.when(part != half)
        def _():
            via_copy().start()

    for i in range(records):
        r = turn(i)
        either(
            o_stays(i),
            lambda: pltpu.make_async_copy(og_source(r), xo.at[me], o_recv_sem.at[me]),
            lambda: o_copy(i),
        )
    by_record(q_in, q_ref)
    x_start(0)
    by_record(k_in, k_ref)
    x_start(1)
    by_record(v_in, v_ref)
    x_start(2)
    for t in range(3):
        w_starts(t, 0)
    shift_og.start()
    shift_li.start()

    @pl.when(via_relays)
    def _():
        for k in range(2):
            remote(
                ow_via.at[k],
                ow_via.at[k],
                via_send_sem.at[0, k],
                via_recv_sem.at[k],
                section,
                me,
            ).wait_recv()
            via_on(k, 1).start()
            via_on(k, 0).start()

    @pl.when(ow_relays)
    def _():
        for k in range(2):
            slot = k * parts + part
            ow_on(slot, 0).wait_recv()
            ow_on(slot, 1).start()
            ow_on(slot, 0).start()

    for k in range(records):
        o_pass(k).wait_recv()
        o_pass(k).start()

    @pl.when(lead)
    def _():
        for t in range(3):
            w_starts(t, 1)

    for slot in range(records):

        @pl.when(jnp.logical_not(ow_relays & (part == slot % parts)))
        def _():
            ow_on(slot, 0).wait_recv()

            @pl.when(lead)
            def _():
                ow_on(slot, 0).start()

    for k in range(records):
        slot = k * parts + 1 - part
        remote(
            xo.at[slot], xo.at[slot], o_pass_sem.at[k], o_recv_sem.at[slot], section, me
        ).wait_recv()

    length = n * frames
    rows_here = ow.shape[1]

    def project(i, carry):
        weight = ow[pl.ds(2 * i, 2)].reshape(2 * rows_here, ow.shape[2])
        grads = xo[...].reshape(length, xo.shape[2])
        lanes = pl.ds(pl.multiple_of(i * 2 * rows_here, 2 * rows_here), 2 * rows_here)
        g[:, lanes] = lax.dot_general(
            grads, weight, ROW_DOT, preferred_element_type=jnp.float32
        ).astype(jnp.bfloat16)
        return carry

    lax.fori_loop(0, cols // (2 * rows_here), project, 0)
    twin_lens.wait_recv()
    twin_gain.wait_recv()
    shift_li.wait_recv()
    width = og_here.shape[1]
    for r in range(records):
        inputs = li_here[:, r, :].astype(jnp.float32)
        centered = inputs - jnp.sum(inputs, axis=1, keepdims=True) * (1.0 / width)
        var = jnp.sum(centered * centered, axis=1, keepdims=True) * (1.0 / width)
        deviation = 1.0 / jnp.sqrt(var + EPSILON)
        normals[r] = centered * deviation
        deviations[r] = jnp.broadcast_to(deviation, deviations.shape[1:])
    for t in range(3):
        for j in range(n):
            remote(
                heads[t][1].at[j],
                heads[t][1].at[j],
                x_send_sem.at[t, 0, 0],
                x_recv_sem.at[t, j],
                section,
                me,
            ).wait_recv()

    valid = jnp.where(lead, lens[0], lens[1])
    valid = jnp.sum(jnp.where(lane == record, valid, 0), axis=1, keepdims=True)[:1]
    keys_ok = lax.broadcasted_iota(jnp.int32, (length, 1), 0) < valid
    low_lanes = lax.broadcasted_iota(jnp.int32, (length, 2 * HS), 1) < HS
    scale = HS ** (-0.5)

    plan = [(0, 0, 0), (0, 0, 1), (0, 0, 2), (1, 1, 0), (1, 1, 1), (1, 1, 2)]
    plan += [(3, 2, 0), (3, 3, 0), (6, 2, 1), (6, 3, 1)]
    steps = 2 * pairs

    def between(step):
        for at in sorted({s for s, _, _ in plan}):

            @pl.when(step == min(at, steps - 1))
            def _():
                for s, i, t in plan:
                    if s == at:
                        w_pass(order(i), t)

    def attend(j, carry):
        lanes = pl.ds(pl.multiple_of(j * 2 * HS, 2 * HS), 2 * HS)
        queries, keys, values = (x[:, :, lanes].reshape(length, 2 * HS) for x in (xq, xk, xv))
        grads = g[:, lanes]
        keys_across = keys.T
        nothing = jnp.zeros_like(keys)
        halves = []
        for h in range(2):
            mine = low_lanes if h == 0 else jnp.logical_not(low_lanes)
            key_h = jnp.where(mine, keys, nothing)
            value_h = jnp.where(mine, values, nothing)
            scores = (
                lax.dot_general(key_h, queries, ROW_DOT, preferred_element_type=jnp.float32)
                * scale
            )
            scores = jnp.where(keys_ok, scores, MASKED)
            weights = jnp.exp(scores - jnp.max(scores, axis=0, keepdims=True))
            probs = weights * (1.0 / jnp.sum(weights, axis=0, keepdims=True))
            grad_probs = lax.dot_general(
                value_h, grads, ROW_DOT, preferred_element_type=jnp.float32
            )
            centre = jnp.sum(probs * grad_probs, axis=0, keepdims=True)
            grad_scores = (probs * (grad_probs - centre)).astype(jnp.bfloat16)
            value_grad = jnp.dot(
                probs.astype(jnp.bfloat16), grads, preferred_element_type=jnp.float32
            )
            key_grad = jnp.dot(grad_scores, queries, preferred_element_type=jnp.float32)
            query_grad = jnp.dot(
                keys_across[h * HS : (h + 1) * HS], grad_scores, preferred_element_type=jnp.float32
            )
            halves.append((query_grad, key_grad, value_grad))
            between(2 * j + h)
        (query_0, key_0, value_0), (query_1, key_1, value_1) = halves
        query_both = (jnp.concatenate([query_0, query_1], axis=0) * scale).T
        key_both = jnp.where(low_lanes, key_0, key_1) * scale
        value_both = jnp.where(low_lanes, value_0, value_1)
        for t, both in enumerate((query_both, key_both, value_both)):
            at = pl.multiple_of(t * cols + j * 2 * HS, 2 * HS)
            joined[:, pl.ds(at, 2 * HS)] = both.astype(jnp.bfloat16)

        return carry

    lax.fori_loop(0, pairs, attend, 0)

    def side_copy(origin):
        other = 1 - part
        return remote(
            part_send.at[origin, other],
            side_recv.at[origin],
            side_send_sem.at[origin],
            side_recv_sem.at[origin],
            section,
            z * parts + other,
        )

    def sum_copy(origin, to):
        return remote(
            sum_send.at[origin, to],
            part_recv.at[record, origin],
            p_send_sem.at[origin, to],
            p_recv_sem.at[record, origin],
            before,
            to * parts + part,
        )

    def sum_stays(to):
        return (before == section) & (to == z)

    def norm_block(origin):
        weight = w[pl.ds(origin * parts, parts)].reshape(parts * w.shape[1], w.shape[2])
        sums = lax.dot_general(
            joined[...], weight, ROW_DOT, preferred_element_type=jnp.float32
        )
        gain = jnp.where(lead, gain_ref[origin], gains[origin])
        sums = (sums * gain).astype(jnp.bfloat16)
        sums = sums.reshape(records, parts, frames, sums.shape[1])
        for other in range(parts):
            part_send[origin, other] = sums[:, other]
        side_copy(origin).start()

    def norm_send(origin):
        side_copy(origin).wait_recv()
        total = part_send[origin, part].astype(jnp.float32)
        total = total + side_recv[origin].astype(jnp.float32)
        sum_send[origin] = total.astype(jnp.bfloat16)
        for k in range(records):
            to = (z + k) % records
            either(
                sum_stays(to),
                lambda: pltpu.make_async_copy(
                    sum_send.at[origin, to],
                    part_recv.at[record, origin],
                    p_recv_sem.at[record, origin],
                ),
                lambda: sum_copy(origin, to),
            )

    def norm(i, carry):
        origin = jnp.where(
            i == 0, order(0), jnp.where(i == 1, order(1), jnp.where(i == 2, order(2), order(3)))
        )
        last = jnp.where(i == 1, order(0), jnp.where(i == 2, order(1), order(2)))

        @pl.when(i == 2)
        def _():
            norm_send(last)
            w_pass(order(2), 2)
            w_pass(order(3), 2)

        norm_block(origin)

        @pl.when((i == 1) | (i == records - 1))
        def _():
            norm_send(last)

        @pl.when(i == records - 1)
        def _():
            norm_send(origin)

        return carry

    lax.fori_loop(0, records, norm, 0)

    shift_og.wait_recv()

    def finish(r):
        rows = pl.ds(r * frames, frames)
        normal = normals[r]
        deviation = deviations[r][:, :1]
        scaled = []
        for origin in range(records):
            remote(
                sum_send.at[origin, 0],
                part_recv.at[r, origin],
                p_send_sem.at[origin, 0],
                p_recv_sem.at[r, origin],
                before,
                me,
            ).wait_recv()
        for origin in range(records):
            scaled.append(part_recv[r, origin].astype(jnp.float32))
        scaled = jnp.concatenate(scaled, axis=1)
        average = jnp.sum(scaled, axis=1, keepdims=True) * (1.0 / width)
        along = jnp.sum(scaled * normal, axis=1, keepdims=True) * (1.0 / width)
        branch = deviation * (scaled - average - normal * along)
        out_ref[rows, :] = (og_here[rows, :].astype(jnp.float32) + branch).astype(jnp.bfloat16)

    for r in range(records):
        finish(r)

    def sent(stays, copy):
        @pl.when(jnp.logical_not(stays))
        def _():
            copy.wait_send()

    twin_lens.wait_send()
    twin_gain.wait_send()
    shift_og.wait_send()
    shift_li.wait_send()
    for i in range(records):
        sent(o_stays(i), o_copy(i))
        o_pass(i).wait_send()
        for t in range(3):
            for p in range(parts):
                sent(x_stays(i, p), x_copy(t, i, p))
    for d in range(2):

        @pl.when(sends(d))
        def _():
            for p in range(parts):
                for t in range(3):
                    sent(w_stays(d, p), w_copy(d, p, t))

        @pl.when(lead)
        def _():
            sent(ow_stays(d), ow_copy(d))

    @pl.when(jnp.logical_not(lead) & (part == half))
    def _():
        near_copy().wait_send()

    @pl.when(jnp.logical_not(lead) & (part != half))
    def _():
        via_copy().wait_send()

    @pl.when(via_relays)
    def _():
        for k in range(2):
            via_on(k, 1).wait_send()
            via_on(k, 0).wait_send()

    for slot in range(records):

        @pl.when(ow_relays & (part == slot % parts))
        def _():
            ow_on(slot, 1).wait_send()

    @pl.when(lead)
    def _():
        for slot in range(records):
            ow_on(slot, 0).wait_send()
        for slot in range(n):
            for t in range(3):
                w_on(slot, t, 0).wait_send()

    for origin in range(records):

        @pl.when(w_relays(origin))
        def _():
            for other in range(parts):
                for t in range(3):
                    w_on(origin * parts + other, t, 1).wait_send()

        side_copy(origin).wait_send()
        for to in range(records):
            sent(sum_stays(to), sum_copy(origin, to))


def on_device_fused(
    layer_input,
    norm_gain,
    queries,
    key_states,
    value_states,
    out_grad,
    out_weight,
    qkv_weight,
    lengths,
):
    n = lax.axis_size("seq")
    sections = lax.axis_size("section")
    frames, records, features = queries.shape[1:]
    width = out_grad.shape[3]
    parts = n // records
    cols = features // parts
    ow_rows = out_weight.shape[1]
    w_rows = qkv_weight.shape[1]
    block = parts * w_rows

    gain = norm_gain[0].reshape(records, 1, block)
    vmem = pl.BlockSpec(memory_space=pltpu.VMEM)
    low = jnp.bfloat16
    dma = pltpu.SemaphoreType.DMA
    out = pl.pallas_call(
        functools.partial(body, (n, sections, records, parts, frames, cols)),
        out_shape=jax.ShapeDtypeStruct((records * frames, width), low),
        in_specs=[pl.BlockSpec(memory_space=pltpu.SMEM)] + [vmem] * 5 + [pl.BlockSpec(memory_space=pl.ANY)] * 2 + [vmem],
        out_specs=vmem,
        scratch_shapes=[pltpu.VMEM((records, frames, features), low)] * 3
        + [pltpu.VMEM((records * frames, width), low)]
        + [pltpu.VMEM((n, frames, cols), low)] * 3
        + [
            pltpu.VMEM((n, frames, width), low),
            pltpu.VMEM((n * frames, cols), low),
            pltpu.VMEM((records, ow_rows, width), low),
            pltpu.VMEM((2, ow_rows, width), low),
            pltpu.VMEM((n, w_rows, 3 * cols), low),
            pltpu.VMEM((n * frames, 3 * cols), low),
            pltpu.VMEM((records, parts, records, frames, block), low),
            pltpu.VMEM((records, records, frames, block), low),
            pltpu.VMEM((records, records, frames, block), low),
            pltpu.VMEM((records, records, frames, block), low),
            pltpu.VMEM((frames, records, width), low),
            pltpu.VMEM((records * frames, width), low),
            pltpu.VMEM((records, frames, width), jnp.float32),
            pltpu.VMEM((records, frames, 128), jnp.float32),
            pltpu.VMEM((2, 8, 128), jnp.int32),
            pltpu.VMEM((records, 1, block), jnp.float32),
            dma((3, records, parts)),
            dma((3, n)),
            dma((records,)),
            dma((records,)),
            dma((n,)),
            dma((2,)),
            dma((2, records)),
            dma((records,)),
            dma((3, 2)),
            dma((2,)),
            dma((2, parts, 3)),
            dma((2, n, 3)),
            dma((n, 3)),
            dma((records,)),
            dma((records,)),
            dma((records, records)),
            dma((records, records)),
            dma((2,)),
            dma((2,)),
            dma((2,)),
            dma((2,)),
        ],
        compiler_params=pltpu.CompilerParams(
            collective_id=0, has_side_effects=True, vmem_limit_bytes=60 * 1024 * 1024
        ),
    )(
        lengths[0],
        layer_input[0],
        queries[0],
        key_states[0],
        value_states[0],
        out_grad[0],
        out_weight[0],
        qkv_weight[0],
        gain,
    )
    return out.reshape(records, frames, width).transpose(1, 0, 2)[None]


def fits(mesh, records, features):
    n = mesh.shape["seq"]
    if n != 2 * records or records != 4 or mesh.shape["section"] % 2:
        return False
    return features % (n * HS) == 0


def solution(mesh):
    in_specs = (
        P("section", "seq", None, None),
        P("section", None),
        P("section", "seq", None, None),
        P("section", "seq", None, None),
        P("section", "seq", None, None),
        P("section", "seq", None, None),
        P("section", "seq", None),
        P("section", "seq", None),
        P("section", None),
    )
    out_specs = P("section", "seq", None, None)

    def run(*arrays):
        fused = fits(mesh, arrays[2].shape[2], arrays[2].shape[3])
        return jax.shard_map(
            on_device_fused if fused else on_device,
            mesh=mesh,
            in_specs=in_specs,
            out_specs=out_specs,
            check_vma=False,
        )(*arrays)

    return run
```

```python
import functools

import jax
import jax.numpy as jnp
from jax import lax
from jax.experimental import pallas as pl
from jax.experimental.pallas import tpu as pltpu
from jax.sharding import PartitionSpec as P

HEADS = 16
HS = 64


EPSILON = 1e-05
MASKED = -1e30
ROW_DOT = (((1,), (1,)), ((), ()))
COL_DOT = (((0,), (0,)), ((), ()))


def shifted(shard, axis, by):
    count = lax.axis_size(axis)
    return lax.ppermute(shard, axis, [(i, (i + by) % count) for i in range(count)])


def item_backward(query_rows, key_rows, value_rows, grad_rows, key_valid):
    length = query_rows.shape[0]
    block = min(512, length)
    scale = HS ** (-0.5)
    offsets = jnp.arange(0, length, block)
    zeros = jnp.zeros((length, query_rows.shape[1]), jnp.float32)

    def step(carry, offset):
        key_total, value_total = carry
        query_block = lax.dynamic_slice_in_dim(query_rows, offset, block, 0)
        grad_block = lax.dynamic_slice_in_dim(grad_rows, offset, block, 0)
        scores = (
            lax.dot_general(query_block, key_rows, ROW_DOT, preferred_element_type=jnp.float32)
            * scale
        )
        scores = jnp.where(key_valid[None, :], scores, MASKED)
        largest = jnp.max(scores, axis=1, keepdims=True)
        weights = jnp.exp(scores - largest)
        probs = weights / jnp.sum(weights, axis=1, keepdims=True)
        probs_low = probs.astype(jnp.bfloat16)
        grad_probs = lax.dot_general(
            grad_block, value_rows, ROW_DOT, preferred_element_type=jnp.float32
        )
        centre = jnp.sum(probs * grad_probs, axis=1, keepdims=True)
        grad_scores = (probs * (grad_probs - centre) * scale).astype(jnp.bfloat16)
        query_grad = jnp.dot(grad_scores, key_rows, preferred_element_type=jnp.float32)
        key_total = key_total + lax.dot_general(
            grad_scores, query_block, COL_DOT, preferred_element_type=jnp.float32
        )
        value_total = value_total + lax.dot_general(
            probs_low, grad_block, COL_DOT, preferred_element_type=jnp.float32
        )
        return ((key_total, value_total), query_grad.astype(jnp.bfloat16))

    (key_total, value_total), query_parts = lax.scan(step, (zeros, zeros), offsets)
    query_grad = query_parts.reshape(length, query_rows.shape[1])
    return (query_grad, key_total.astype(jnp.bfloat16), value_total.astype(jnp.bfloat16))


def split_items(columns):
    length = columns.shape[0]
    count = columns.shape[1] // HS
    return columns.reshape(length, count, HS).transpose(1, 0, 2)


def join_items(items):
    count = items.shape[0]
    length = items.shape[1]
    return items.transpose(1, 0, 2).reshape(length, count * HS)


def project_grad(flat_grad, out_rows):
    return lax.dot_general(
        flat_grad,
        lax.all_gather(out_rows, "seq", axis=0, tiled=True),
        ROW_DOT,
        preferred_element_type=jnp.float32,
    ).astype(jnp.bfloat16)


def on_device(
    layer_input,
    norm_gain,
    queries,
    key_states,
    value_states,
    out_grad,
    out_weight,
    qkv_weight,
    lengths,
):
    frames = queries.shape[1]
    records = queries.shape[2]
    features = queries.shape[3]
    model_width = out_grad.shape[3]
    flat_grad = out_grad[0].reshape(frames * records, model_width)
    frame_queries = queries[0].reshape(frames, records * features)
    frame_keys = key_states[0].reshape(frames, records * features)
    frame_values = value_states[0].reshape(frames, records * features)
    attn_grad = project_grad(flat_grad, out_weight[0])
    head_queries, head_keys, head_values, head_grads = (
        lax.all_to_all(frame_queries, "seq", split_axis=1, concat_axis=0, tiled=True),
        lax.all_to_all(frame_keys, "seq", split_axis=1, concat_axis=0, tiled=True),
        lax.all_to_all(frame_values, "seq", split_axis=1, concat_axis=0, tiled=True),
        lax.all_to_all(
            attn_grad.reshape(frames, records * features),
            "seq",
            split_axis=1,
            concat_axis=0,
            tiled=True,
        ),
    )
    items_here = head_queries.shape[1] // HS
    length = head_queries.shape[0]
    item_ids = lax.axis_index("seq") * items_here + jnp.arange(items_here, dtype=jnp.int32)
    record_ids = item_ids // HEADS
    record_pick = jnp.arange(records, dtype=jnp.int32)[None, :] == record_ids[:, None]
    item_lengths = jnp.sum(jnp.where(record_pick, lengths[0][None, :], 0), axis=1)
    key_valid = jnp.arange(length, dtype=jnp.int32)[None, :] < item_lengths[:, None]
    query_grad, key_gradient, value_grad = lax.map(
        lambda group: item_backward(*group),
        (
            split_items(head_queries),
            split_items(head_keys),
            split_items(head_values),
            split_items(head_grads),
            key_valid,
        ),
    )
    query_back, key_backward, value_back = (
        lax.all_to_all(join_items(query_grad), "seq", split_axis=0, concat_axis=1, tiled=True),
        lax.all_to_all(join_items(key_gradient), "seq", split_axis=0, concat_axis=1, tiled=True),
        lax.all_to_all(join_items(value_grad), "seq", split_axis=0, concat_axis=1, tiled=True),
    )
    joined = jnp.concatenate(
        [
            query_back.reshape(frames * records, features),
            key_backward.reshape(frames * records, features),
            value_back.reshape(frames * records, features),
        ],
        axis=1,
    )
    norm_grad = lax.dot_general(
        joined,
        lax.all_gather(qkv_weight[0], "seq", axis=0, tiled=True),
        ROW_DOT,
        preferred_element_type=jnp.float32,
    )
    inputs = layer_input[0].reshape(frames * records, model_width).astype(jnp.float32)
    row_average = jnp.mean(inputs, axis=1, keepdims=True)
    centered_input = inputs - row_average
    var = jnp.mean(centered_input * centered_input, axis=1, keepdims=True)
    inverse_deviation = 1.0 / jnp.sqrt(var + EPSILON)
    normalized_input = centered_input * inverse_deviation
    scaled_rows = norm_grad * norm_gain[0][None, :]
    residual_branch = inverse_deviation * (
        scaled_rows
        - jnp.mean(scaled_rows, axis=1, keepdims=True)
        - normalized_input * jnp.mean(scaled_rows * normalized_input, axis=1, keepdims=True)
    )
    input_grad = (flat_grad.astype(jnp.float32) + residual_branch).astype(jnp.bfloat16)
    input_grad = input_grad.reshape(1, frames, records, model_width)
    return shifted(input_grad, "section", -1)


def body(
    dims,
    length_ref,
    li_ref,
    q_in,
    k_in,
    v_in,
    og_in,
    ow_in,
    w_in,
    gain_ref,
    out_ref,
    q_ref,
    k_ref,
    v_ref,
    og_ref,
    xq,
    xk,
    xv,
    xo,
    g,
    ow,
    ow_via,
    w,
    joined,
    part_send,
    side_recv,
    sum_send,
    part_recv,
    li_here,
    og_here,
    normals,
    deviations,
    lens,
    gains,
    x_send_sem,
    x_recv_sem,
    o_send_sem,
    o_pass_sem,
    o_recv_sem,
    ow_send_sem,
    ow_pass_sem,
    ow_recv_sem,
    via_send_sem,
    via_recv_sem,
    w_send_sem,
    w_pass_sem,
    w_recv_sem,
    side_send_sem,
    side_recv_sem,
    p_send_sem,
    p_recv_sem,
    s_send_sem,
    s_recv_sem,
    twin_send_sem,
    twin_recv_sem,
):
    n, sections, records, parts, frames, cols = dims
    pairs = cols // (2 * HS)
    section = lax.axis_index("section")
    me = lax.axis_index("seq")
    core = section % 2
    z = me // parts
    part = me % parts
    half = z // 2
    twin = section + 1 - 2 * core
    work = section - core + half
    record = 2 * (z % 2) + core
    lead = core == half
    near = z == 1 + half
    prior = (section + sections - 1) % sections
    before = (work + sections - 1) % sections

    def remote(src, dst, send, recv, sec, dev):
        return pltpu.make_async_remote_copy(
            src_ref=src,
            dst_ref=dst,
            send_sem=send,
            recv_sem=recv,
            device_id=(sec, dev),
            device_id_type=pl.DeviceIdType.MESH,
        )

    def either(stays, copy_here, copy_there):
        @pl.when(stays)
        def _():
            copy_here().start()

        @pl.when(jnp.logical_not(stays))
        def _():
            copy_there().start()

    barrier = pltpu.get_barrier_semaphore()
    for s in range(sections):
        for k in range(n):
            if s or k:
                pl.semaphore_signal(
                    barrier,
                    inc=1,
                    device_id=((section + s) % sections, (me + k) % n),
                    device_id_type=pl.DeviceIdType.MESH,
                )

    lane = lax.broadcasted_iota(jnp.int32, lens.shape[1:], 1)
    lengths = jnp.zeros(lens.shape[1:], jnp.int32)
    for r in range(records):
        lengths = jnp.where(lane == r, length_ref[r], lengths)
    lens[0] = lengths

    def by_record(source, target):
        for r in range(records):
            if len(target.shape) == 2:
                target[r * frames : (r + 1) * frames] = source[:, r, :]
            else:
                target[r] = source[:, r, :]

    by_record(og_in, og_ref)
    pl.semaphore_wait(barrier, sections * n - 1)

    twin_lens = remote(lens.at[0], lens.at[1], twin_send_sem.at[0], twin_recv_sem.at[0], twin, me)
    twin_gain = remote(gain_ref, gains, twin_send_sem.at[1], twin_recv_sem.at[1], twin, me)

    def seat(r, p):
        return section - core + r % 2, (2 * core + r // 2) * parts + p

    def turn(i):
        return (i + 2 * core) % records

    heads = [(q_ref, xq), (k_ref, xk), (v_ref, xv)]

    def x_source(t, r, p):
        return heads[t][0].at[r, :, pl.ds(p * cols, cols)]

    def x_copy(t, i, p):
        r = turn(i)
        sec, dev = seat(r, p)
        return remote(
            x_source(t, r, p),
            heads[t][1].at[me],
            x_send_sem.at[t, i, p],
            x_recv_sem.at[t, me],
            sec,
            dev,
        )

    def x_stays(i, p):
        return lead & (turn(i) == record) & (part == p)

    def x_start(t):
        for i in range(records):
            for p in range(parts):
                either(
                    x_stays(i, p),
                    lambda: pltpu.make_async_copy(
                        x_source(t, turn(i), p), heads[t][1].at[me], x_recv_sem.at[t, me]
                    ),
                    lambda: x_copy(t, i, p),
                )

    def og_source(r):
        return og_ref.at[pl.ds(pl.multiple_of(r * frames, frames), frames)]

    def o_copy(i):
        r = turn(i)
        sec, dev = seat(r, part)
        return remote(og_source(r), xo.at[me], o_send_sem.at[i], o_recv_sem.at[me], sec, dev)

    def o_stays(i):
        return lead & (turn(i) == record)

    def o_pass(k):
        slot = k * parts + part
        return remote(
            xo.at[slot],
            xo.at[slot],
            o_pass_sem.at[k],
            o_recv_sem.at[slot],
            section,
            z * parts + 1 - part,
        )

    def lead_z(d):
        return 1 + core if d == 0 else 3 * core

    ow_slot = me % records

    def ow_copy(d):
        return remote(
            ow_in,
            ow.at[ow_slot],
            ow_send_sem.at[d],
            ow_recv_sem.at[ow_slot],
            section,
            lead_z(d) * parts + half,
        )

    through = part != half

    def via_copy():
        return remote(
            ow_in,
            ow_via.at[z % 2],
            via_send_sem.at[0, 0],
            via_recv_sem.at[z % 2],
            section,
            (1 + core) * parts + part,
        )

    def via_on(k, way):
        slot = k * parts + part
        dev = (1 + half if way == 0 else 3 * half) * parts + 1 - half
        return remote(
            ow_via.at[k],
            ow.at[slot],
            via_send_sem.at[1 + way, k],
            ow_recv_sem.at[slot],
            section,
            dev,
        )

    def near_copy():
        return remote(
            ow_in,
            ow.at[ow_slot],
            ow_send_sem.at[0],
            ow_recv_sem.at[ow_slot],
            section,
            (1 + core) * parts + part,
        )

    def ow_stays(d):
        return (lead_z(d) == z) & (part == half)

    def w_source(t, p):
        return w_in.at[:, pl.ds(pl.multiple_of((t * parts + p) * cols, cols), cols)]

    def w_target(t):
        return w.at[me, :, pl.ds(t * cols, cols)]

    def w_copy(d, p, t):
        return remote(
            w_source(t, p),
            w_target(t),
            w_send_sem.at[d, p, t],
            w_recv_sem.at[me, t],
            section,
            lead_z(d) * parts + p,
        )

    def w_stays(d, p):
        return (lead_z(d) == z) & (part == p)

    def sends(d):
        return lead | (d == 0)

    def ow_start(d):
        either(
            ow_stays(d),
            lambda: pltpu.make_async_copy(ow_in, ow.at[ow_slot], ow_recv_sem.at[ow_slot]),
            lambda: ow_copy(d),
        )

    def w_start(t, d, p):
        either(
            w_stays(d, p),
            lambda: pltpu.make_async_copy(w_source(t, p), w_target(t), w_recv_sem.at[me, t]),
            lambda: w_copy(d, p, t),
        )

    def w_starts(t, d):
        for q in range(parts):
            p = (part + q) % parts
            w_start(t, d, p)

    def ow_on(slot, way):
        sec, dev = (twin, me) if way == 0 else (section, 3 * half * parts + part)
        return remote(
            ow.at[slot], ow.at[slot], ow_pass_sem.at[way, slot], ow_recv_sem.at[slot], sec, dev
        )

    def w_on(slot, t, way):
        sec, dev = (twin, me) if way == 0 else (section, 3 * half * parts + part)
        at = w.at[slot, :, pl.ds(t * cols, cols)]
        return remote(at, at, w_pass_sem.at[way, slot, t], w_recv_sem.at[slot, t], sec, dev)

    relays = lead & near
    ow_relays = relays & (part != half)
    via_relays = relays & (part == half)

    def w_relays(origin):
        return lead & near & (origin // 2 != half)

    def w_pass(origin, t):
        for q in range(parts):
            slot = origin * parts + (part + q) % parts
            w_on(slot, t, 0).wait_recv()

            @pl.when(w_relays(origin))
            def _():
                w_on(slot, t, 1).start()

            @pl.when(lead)
            def _():
                w_on(slot, t, 0).start()

    def order(i):
        return (z, 2 * half + 1 - z % 2, 2 - half, 3 - 3 * half)[i]

    shift_og = remote(og_ref, og_here, s_send_sem.at[0], s_recv_sem.at[0], prior, me)
    shift_li = remote(li_ref, li_here, s_send_sem.at[1], s_recv_sem.at[1], prior, me)

    twin_lens.start()
    twin_gain.start()
    @pl.when(lead)
    def _():
        ow_start(0)
        ow_start(1)

    @pl.when(jnp.logical_not(lead))
    def _():
        @pl.when(part == half)
        def _():
            near_copy().start()

        @pl.when(part != half)
        def _():
            via_copy().start()

    for i in range(records):
        r = turn(i)
        either(
            o_stays(i),
            lambda: pltpu.make_async_copy(og_source(r), xo.at[me], o_recv_sem.at[me]),
            lambda: o_copy(i),
        )
    by_record(q_in, q_ref)
    x_start(0)
    by_record(k_in, k_ref)
    x_start(1)
    by_record(v_in, v_ref)
    x_start(2)
    for t in range(3):
        w_starts(t, 0)
    shift_og.start()
    shift_li.start()

    @pl.when(via_relays)
    def _():
        for k in range(2):
            remote(
                ow_via.at[k],
                ow_via.at[k],
                via_send_sem.at[0, k],
                via_recv_sem.at[k],
                section,
                me,
            ).wait_recv()
            via_on(k, 1).start()
            via_on(k, 0).start()

    @pl.when(ow_relays)
    def _():
        for k in range(2):
            slot = k * parts + part
            ow_on(slot, 0).wait_recv()
            ow_on(slot, 1).start()
            ow_on(slot, 0).start()

    for k in range(records):
        o_pass(k).wait_recv()
        o_pass(k).start()

    @pl.when(lead)
    def _():
        for t in range(3):
            w_starts(t, 1)

    for slot in range(records):

        @pl.when(jnp.logical_not(ow_relays & (part == slot % parts)))
        def _():
            ow_on(slot, 0).wait_recv()

            @pl.when(lead)
            def _():
                ow_on(slot, 0).start()

    for k in range(records):
        slot = k * parts + 1 - part
        remote(
            xo.at[slot], xo.at[slot], o_pass_sem.at[k], o_recv_sem.at[slot], section, me
        ).wait_recv()

    length = n * frames
    rows_here = ow.shape[1]

    def project(i, carry):
        weight = ow[pl.ds(2 * i, 2)].reshape(2 * rows_here, ow.shape[2])
        grads = xo[...].reshape(length, xo.shape[2])
        lanes = pl.ds(pl.multiple_of(i * 2 * rows_here, 2 * rows_here), 2 * rows_here)
        g[:, lanes] = lax.dot_general(
            grads, weight, ROW_DOT, preferred_element_type=jnp.float32
        ).astype(jnp.bfloat16)
        return carry

    lax.fori_loop(0, cols // (2 * rows_here), project, 0)
    twin_lens.wait_recv()
    twin_gain.wait_recv()
    shift_li.wait_recv()
    width = og_here.shape[1]
    for r in range(records):
        inputs = li_here[:, r, :].astype(jnp.float32)
        centered = inputs - jnp.sum(inputs, axis=1, keepdims=True) * (1.0 / width)
        var = jnp.sum(centered * centered, axis=1, keepdims=True) * (1.0 / width)
        deviation = 1.0 / jnp.sqrt(var + EPSILON)
        normals[r] = centered * deviation
        deviations[r] = jnp.broadcast_to(deviation, deviations.shape[1:])
    for t in range(3):
        for j in range(n):
            remote(
                heads[t][1].at[j],
                heads[t][1].at[j],
                x_send_sem.at[t, 0, 0],
                x_recv_sem.at[t, j],
                section,
                me,
            ).wait_recv()

    valid = jnp.where(lead, lens[0], lens[1])
    valid = jnp.sum(jnp.where(lane == record, valid, 0), axis=1, keepdims=True)[:1]
    keys_ok = lax.broadcasted_iota(jnp.int32, (length, 1), 0) < valid
    low_lanes = lax.broadcasted_iota(jnp.int32, (length, 2 * HS), 1) < HS
    scale = HS ** (-0.5)

    plan = [(0, 0, 0), (0, 0, 1), (0, 0, 2), (1, 1, 0), (1, 1, 1), (1, 1, 2)]
    plan += [(3, 2, 0), (3, 3, 0), (6, 2, 1), (6, 3, 1)]
    steps = 2 * pairs

    def between(step):
        for at in sorted({s for s, _, _ in plan}):

            @pl.when(step == min(at, steps - 1))
            def _():
                for s, i, t in plan:
                    if s == at:
                        w_pass(order(i), t)

    def attend(j, carry):
        lanes = pl.ds(pl.multiple_of(j * 2 * HS, 2 * HS), 2 * HS)
        queries, keys, values = (x[:, :, lanes].reshape(length, 2 * HS) for x in (xq, xk, xv))
        grads = g[:, lanes]
        keys_across = keys.T
        nothing = jnp.zeros_like(keys)
        halves = []
        for h in range(2):
            mine = low_lanes if h == 0 else jnp.logical_not(low_lanes)
            key_h = jnp.where(mine, keys, nothing)
            value_h = jnp.where(mine, values, nothing)
            scores = (
                lax.dot_general(key_h, queries, ROW_DOT, preferred_element_type=jnp.float32)
                * scale
            )
            scores = jnp.where(keys_ok, scores, MASKED)
            weights = jnp.exp(scores - jnp.max(scores, axis=0, keepdims=True))
            probs = weights * (1.0 / jnp.sum(weights, axis=0, keepdims=True))
            grad_probs = lax.dot_general(
                value_h, grads, ROW_DOT, preferred_element_type=jnp.float32
            )
            centre = jnp.sum(probs * grad_probs, axis=0, keepdims=True)
            grad_scores = (probs * (grad_probs - centre)).astype(jnp.bfloat16)
            value_grad = jnp.dot(
                probs.astype(jnp.bfloat16), grads, preferred_element_type=jnp.float32
            )
            key_grad = jnp.dot(grad_scores, queries, preferred_element_type=jnp.float32)
            query_grad = jnp.dot(
                keys_across[h * HS : (h + 1) * HS], grad_scores, preferred_element_type=jnp.float32
            )
            halves.append((query_grad, key_grad, value_grad))
            between(2 * j + h)
        (query_0, key_0, value_0), (query_1, key_1, value_1) = halves
        query_both = (jnp.concatenate([query_0, query_1], axis=0) * scale).T
        key_both = jnp.where(low_lanes, key_0, key_1) * scale
        value_both = jnp.where(low_lanes, value_0, value_1)
        for t, both in enumerate((query_both, key_both, value_both)):
            at = pl.multiple_of(t * cols + j * 2 * HS, 2 * HS)
            joined[:, pl.ds(at, 2 * HS)] = both.astype(jnp.bfloat16)

        return carry

    lax.fori_loop(0, pairs, attend, 0)

    def side_copy(origin):
        other = 1 - part
        return remote(
            part_send.at[origin, other],
            side_recv.at[origin],
            side_send_sem.at[origin],
            side_recv_sem.at[origin],
            section,
            z * parts + other,
        )

    def sum_copy(origin, to):
        return remote(
            sum_send.at[origin, to],
            part_recv.at[record, origin],
            p_send_sem.at[origin, to],
            p_recv_sem.at[record, origin],
            before,
            to * parts + part,
        )

    def sum_stays(to):
        return (before == section) & (to == z)

    def norm_block(origin):
        weight = w[pl.ds(origin * parts, parts)].reshape(parts * w.shape[1], w.shape[2])
        sums = lax.dot_general(
            joined[...], weight, ROW_DOT, preferred_element_type=jnp.float32
        )
        gain = jnp.where(lead, gain_ref[origin], gains[origin])
        sums = (sums * gain).astype(jnp.bfloat16)
        sums = sums.reshape(records, parts, frames, sums.shape[1])
        for other in range(parts):
            part_send[origin, other] = sums[:, other]
        side_copy(origin).start()

    def norm_send(origin):
        side_copy(origin).wait_recv()
        total = part_send[origin, part].astype(jnp.float32)
        total = total + side_recv[origin].astype(jnp.float32)
        sum_send[origin] = total.astype(jnp.bfloat16)
        for k in range(records):
            to = (z + k) % records
            either(
                sum_stays(to),
                lambda: pltpu.make_async_copy(
                    sum_send.at[origin, to],
                    part_recv.at[record, origin],
                    p_recv_sem.at[record, origin],
                ),
                lambda: sum_copy(origin, to),
            )

    def norm(i, carry):
        origin = jnp.where(
            i == 0, order(0), jnp.where(i == 1, order(1), jnp.where(i == 2, order(2), order(3)))
        )
        last = jnp.where(i == 1, order(0), jnp.where(i == 2, order(1), order(2)))

        @pl.when(i == 2)
        def _():
            norm_send(last)
            w_pass(order(2), 2)

        @pl.when(i == records - 1)
        def _():
            w_pass(order(3), 2)

        norm_block(origin)

        @pl.when((i == 1) | (i == records - 1))
        def _():
            norm_send(last)

        @pl.when(i == records - 1)
        def _():
            norm_send(origin)

        return carry

    lax.fori_loop(0, records, norm, 0)

    shift_og.wait_recv()

    def finish(r):
        rows = pl.ds(r * frames, frames)
        normal = normals[r]
        deviation = deviations[r][:, :1]
        scaled = []
        for origin in range(records):
            remote(
                sum_send.at[origin, 0],
                part_recv.at[r, origin],
                p_send_sem.at[origin, 0],
                p_recv_sem.at[r, origin],
                before,
                me,
            ).wait_recv()
        for origin in range(records):
            scaled.append(part_recv[r, origin].astype(jnp.float32))
        scaled = jnp.concatenate(scaled, axis=1)
        average = jnp.sum(scaled, axis=1, keepdims=True) * (1.0 / width)
        along = jnp.sum(scaled * normal, axis=1, keepdims=True) * (1.0 / width)
        branch = deviation * (scaled - average - normal * along)
        out_ref[rows, :] = (og_here[rows, :].astype(jnp.float32) + branch).astype(jnp.bfloat16)

    for r in range(records):
        finish(r)

    def sent(stays, copy):
        @pl.when(jnp.logical_not(stays))
        def _():
            copy.wait_send()

    twin_lens.wait_send()
    twin_gain.wait_send()
    shift_og.wait_send()
    shift_li.wait_send()
    for i in range(records):
        sent(o_stays(i), o_copy(i))
        o_pass(i).wait_send()
        for t in range(3):
            for p in range(parts):
                sent(x_stays(i, p), x_copy(t, i, p))
    for d in range(2):

        @pl.when(sends(d))
        def _():
            for p in range(parts):
                for t in range(3):
                    sent(w_stays(d, p), w_copy(d, p, t))

        @pl.when(lead)
        def _():
            sent(ow_stays(d), ow_copy(d))

    @pl.when(jnp.logical_not(lead) & (part == half))
    def _():
        near_copy().wait_send()

    @pl.when(jnp.logical_not(lead) & (part != half))
    def _():
        via_copy().wait_send()

    @pl.when(via_relays)
    def _():
        for k in range(2):
            via_on(k, 1).wait_send()
            via_on(k, 0).wait_send()

    for slot in range(records):

        @pl.when(ow_relays & (part == slot % parts))
        def _():
            ow_on(slot, 1).wait_send()

    @pl.when(lead)
    def _():
        for slot in range(records):
            ow_on(slot, 0).wait_send()
        for slot in range(n):
            for t in range(3):
                w_on(slot, t, 0).wait_send()

    for origin in range(records):

        @pl.when(w_relays(origin))
        def _():
            for other in range(parts):
                for t in range(3):
                    w_on(origin * parts + other, t, 1).wait_send()

        side_copy(origin).wait_send()
        for to in range(records):
            sent(sum_stays(to), sum_copy(origin, to))


def on_device_fused(
    layer_input,
    norm_gain,
    queries,
    key_states,
    value_states,
    out_grad,
    out_weight,
    qkv_weight,
    lengths,
):
    n = lax.axis_size("seq")
    sections = lax.axis_size("section")
    frames, records, features = queries.shape[1:]
    width = out_grad.shape[3]
    parts = n // records
    cols = features // parts
    ow_rows = out_weight.shape[1]
    w_rows = qkv_weight.shape[1]
    block = parts * w_rows

    gain = norm_gain[0].reshape(records, 1, block)
    vmem = pl.BlockSpec(memory_space=pltpu.VMEM)
    low = jnp.bfloat16
    dma = pltpu.SemaphoreType.DMA
    out = pl.pallas_call(
        functools.partial(body, (n, sections, records, parts, frames, cols)),
        out_shape=jax.ShapeDtypeStruct((records * frames, width), low),
        in_specs=[pl.BlockSpec(memory_space=pltpu.SMEM)] + [vmem] * 5 + [pl.BlockSpec(memory_space=pl.ANY)] * 2 + [vmem],
        out_specs=vmem,
        scratch_shapes=[pltpu.VMEM((records, frames, features), low)] * 3
        + [pltpu.VMEM((records * frames, width), low)]
        + [pltpu.VMEM((n, frames, cols), low)] * 3
        + [
            pltpu.VMEM((n, frames, width), low),
            pltpu.VMEM((n * frames, cols), low),
            pltpu.VMEM((records, ow_rows, width), low),
            pltpu.VMEM((2, ow_rows, width), low),
            pltpu.VMEM((n, w_rows, 3 * cols), low),
            pltpu.VMEM((n * frames, 3 * cols), low),
            pltpu.VMEM((records, parts, records, frames, block), low),
            pltpu.VMEM((records, records, frames, block), low),
            pltpu.VMEM((records, records, frames, block), low),
            pltpu.VMEM((records, records, frames, block), low),
            pltpu.VMEM((frames, records, width), low),
            pltpu.VMEM((records * frames, width), low),
            pltpu.VMEM((records, frames, width), jnp.float32),
            pltpu.VMEM((records, frames, 128), jnp.float32),
            pltpu.VMEM((2, 8, 128), jnp.int32),
            pltpu.VMEM((records, 1, block), jnp.float32),
            dma((3, records, parts)),
            dma((3, n)),
            dma((records,)),
            dma((records,)),
            dma((n,)),
            dma((2,)),
            dma((2, records)),
            dma((records,)),
            dma((3, 2)),
            dma((2,)),
            dma((2, parts, 3)),
            dma((2, n, 3)),
            dma((n, 3)),
            dma((records,)),
            dma((records,)),
            dma((records, records)),
            dma((records, records)),
            dma((2,)),
            dma((2,)),
            dma((2,)),
            dma((2,)),
        ],
        compiler_params=pltpu.CompilerParams(
            collective_id=0, has_side_effects=True, vmem_limit_bytes=60 * 1024 * 1024
        ),
    )(
        lengths[0],
        layer_input[0],
        queries[0],
        key_states[0],
        value_states[0],
        out_grad[0],
        out_weight[0],
        qkv_weight[0],
        gain,
    )
    return out.reshape(records, frames, width).transpose(1, 0, 2)[None]


def fits(mesh, records, features):
    n = mesh.shape["seq"]
    if n != 2 * records or records != 4 or mesh.shape["section"] % 2:
        return False
    return features % (n * HS) == 0


def solution(mesh):
    in_specs = (
        P("section", "seq", None, None),
        P("section", None),
        P("section", "seq", None, None),
        P("section", "seq", None, None),
        P("section", "seq", None, None),
        P("section", "seq", None, None),
        P("section", "seq", None),
        P("section", "seq", None),
        P("section", None),
    )
    out_specs = P("section", "seq", None, None)

    def run(*arrays):
        fused = fits(mesh, arrays[2].shape[2], arrays[2].shape[3])
        return jax.shard_map(
            on_device_fused if fused else on_device,
            mesh=mesh,
            in_specs=in_specs,
            out_specs=out_specs,
            check_vma=False,
        )(*arrays)

    return run
```
